128 devices in a mesh: leaf: 128 (over y, z, x, core).
Axes of the slice: x: 4, y: 4, z: 4, core: 2. Of those that a mesh axis runs over, the one named last changes fastest.
Arguments:
- density: bfloat16 [131072, 220], P('leaf'), may hold values from -6 to 6
- vel_mask: int32 [131072], P('leaf'), may hold values from 0 to 1, as said below
- near_list: int32 [131072, 27], P('leaf'), may hold values from 0 to 131071, as said below
- near_ops: bfloat16 [27, 220, 660], replicated, may hold values from -0.078125 to 0.078125
- upward_ops: bfloat16 [8, 220, 56], replicated, may hold values from -0.0068359375 to 0.0068359375
- coupling_operators: float32 [56, 168], replicated, may hold values from -0.75 to 0.75
- coarse_weights: float32 [32, 32], replicated, may hold values from -1 to 1
- downward_ops: bfloat16 [8, 56, 220], replicated, may hold values from -0.75 to 0.75
- conc_owner: int32 [131072, 1], P('leaf'), may hold values from 0 to 127; in each aligned block of 1024 rows (0 to 1023, 1024 to 2047, ...) at most 16 rows name the same one
- concentration: bfloat16 [262144, 220], P('leaf'), may hold values from -6 to 6
- departure: int32 [262144], P('leaf'), may hold values from 0 to 2047
- departure_class: int32 [262144], P('leaf'), may hold values from 0 to 7
- shift_ops: bfloat16 [8, 220, 220], replicated, may hold values from -0.4375 to 0.4375
- eval_ops: bfloat16 [220, 1024], replicated, may hold values from -0.4375 to 0.4375
Outputs:
- velocity: bfloat16 [131072, 660], P('leaf')
- advected: bfloat16 [262144, 256], P('leaf')
The draws below stay inside these ranges and needn't reach their ends.
Inputs may be any that keep to these rules, and one draw needn't show every extreme that they name: `vel_mask`: in each aligned block of 1024 rows the real leaves come first; every block has from 341 to 1024 real leaves, and both counts occur in every draw. `near_list`: entry [i, t] lies within 1024 of i; column 13 is i itself. `conc_owner`: in each aligned block of 1024 rows, the rows of one device, no owner is named more than 16 times, a bound that some block reaches. `departure`: A slot index within the same device's 2048 slots.
All inputs are finite; a program needn't handle non-finite values.
Results may differ from the reference program's by a relative error of at most 0.008.
Values may be sent and summed in bfloat16 or wider, within the bound.
No kernel may reach another device: no remote copies, remote signals or barrier semaphores. Data moves between devices by JAX's collectives and lax.ppermute only.
A program may use at most 128 MiB of HBM per device.

```python
import math
import jax
import jax.numpy as jnp
import numpy as np
from jax import lax

P_SIZE = 220
Q = 56
NEAR = 27
NODES = 256
NCLS = 8
SPAN = 4
L_DEV = 1024
LEAVES = 131072
CAP = 16
SLOTS_DEV = 2048
SLOTS = 262144
NC = 32
BOX_LEAVES = 4096
N_LEAF = 128


def draw_vel_mask(key, part):
    blocks = LEAVES // L_DEV
    first_key, second_key = jax.random.split(jax.random.fold_in(key, 11))
    counts = jax.random.randint(first_key, (blocks,), L_DEV // 3, L_DEV + 1, dtype=jnp.int32)
    shuffled = jax.random.permutation(second_key, blocks)
    counts = counts.at[shuffled[0]].set(L_DEV).at[shuffled[1]].set(L_DEV // 3)
    point_location = jnp.arange(LEAVES, dtype=jnp.int32)
    return (point_location % L_DEV < counts[point_location // L_DEV]).astype(jnp.int32)


def draw_near_list(key, part):
    offsets = jax.random.randint(jax.random.fold_in(key, 23), (LEAVES, NEAR), -L_DEV, L_DEV + 1, dtype=jnp.int32)
    offsets = offsets.at[:, NEAR // 2].set(0)
    point_location = jnp.arange(LEAVES, dtype=jnp.int32)
    return jnp.clip(point_location[:, None] + offsets, 0, LEAVES - 1).astype(jnp.int32)


def with_ends(entries, stream_key, smallest, top_value):
    dims = entries.shape
    index_at = [jax.random.randint(jax.random.fold_in(stream_key, axis), (), 0, dims[axis]) for axis in range(len(dims))]
    entries = entries.at[tuple(index_at)].set(smallest)
    longest = dims.index(max(dims))
    index_at[longest] = (index_at[longest] + 1) % dims[longest]
    return entries.at[tuple(index_at)].set(top_value)


def shard_levels(rng, extent, shards, low, top_value):
    level = 1.0
    for dim, blocks in shards:
        steps = jax.random.uniform(jax.random.fold_in(jax.random.fold_in(rng, 6), dim), (blocks,), jnp.float32, low / len(shards), top_value / len(shards))
        level = level * jnp.repeat(jnp.exp(steps), extent[dim] // blocks).reshape((-1,) + (1,) * (len(extent) - 1 - dim))
    return level


def routed_block(stream_key, own, number, rows, amount, top, limit, skew):
    ranking = jax.random.permutation(stream_key, amount)
    crowded, ordinary = shares(amount, rows * top, limit, skew, True), shares(amount, rows * top, limit, skew, False)
    places = jnp.arange(amount)

    def named(sizes, turn):
        used = int((sizes > 0).sum())
        fixed = max(1, used // 4)
        passed = fixed + (places - fixed + turn * (used - fixed)) % max(1, amount - fixed)
        return jnp.zeros((amount,), jnp.int32).at[ranking[jnp.where(places < fixed, places, passed)]].set(jnp.asarray(sizes, jnp.int32))

    sizes = jnp.where(number % 4 == 0, named(crowded, number // 4), named(ordinary, number - number // 4 - 1))
    mixed = jax.random.permutation(jax.random.fold_in(own, 3), amount)
    giver, taker = mixed[0:amount // 2 * 2:2], mixed[1:amount // 2 * 2:2]
    slack = jnp.minimum(sizes[giver] - 1, limit - sizes[taker]) // 2
    slack = jnp.where((giver == ranking[0]) | (taker == ranking[0]) | (sizes[taker] == 0), 0, jnp.maximum(slack, 0))
    passed = jax.random.randint(jax.random.fold_in(own, 4), (amount // 2,), 0, 1 << 20) % (slack + 1)
    sizes = sizes.at[giver].add(-passed).at[taker].add(passed)
    items = jnp.searchsorted(jnp.cumsum(sizes), jnp.arange(rows * top), side="right").astype(jnp.int32)
    grid = items.reshape(top, rows).T
    grid = grid[jax.random.permutation(jax.random.fold_in(own, 1), rows)]
    turn = jax.random.randint(jax.random.fold_in(own, 2), (rows, 1), 0, top)
    return jnp.take_along_axis(grid, (jnp.arange(top)[None, :] + turn) % top, axis=1)


def shares(number_of, total, limit, lean, full):
    loads = [(1 << 20) // math.isqrt(grade ** lean) + 1 for grade in range(1, number_of + 1)]
    largest = limit if full else min(limit, max(-(-total // number_of), total * loads[0] // sum(loads)))
    least = 1 if total - largest >= number_of - 1 else 0
    given, spare = [largest] + [least] * (number_of - 1), total - largest - least * (number_of - 1)
    while spare > 0:
        free = [i for i in range(1, number_of) if given[i] < largest] or [i for i in range(1, number_of) if given[i] < limit]
        pool, left = sum([loads[i] for i in free]), spare
        for i in free:
            extra = min(limit - given[i], max(1, left * loads[i] // pool), spare)
            given[i] = given[i] + extra
            spare = spare - extra
    return np.array(given)


def normal_values(key, shape, width, bound, pieces=(), kind=jnp.bfloat16):
    values = width * jax.random.normal(key, shape, jnp.float32)
    if pieces:
        values = values * shard_levels(key, shape, pieces, -0.22, 0.18)
    return jnp.clip(values, -bound, bound).astype(kind)


def setup_inputs(seed: int = 0) -> dict:
    key_of = jax.random.split(jax.random.key(seed), 15)
    density = normal_values(key_of[0], (LEAVES, P_SIZE), 1.0, 6.0, ((0, 128),))
    vel_mask = draw_vel_mask(jax.random.fold_in(key_of[14], 71), 0)
    near_list = draw_near_list(jax.random.fold_in(key_of[14], 71), 0)
    near_ops = normal_values(key_of[3], (NEAR, P_SIZE, 3 * P_SIZE), (NEAR * P_SIZE) ** -0.5, 0.078125)
    upward_ops = normal_values(key_of[4], (8, P_SIZE, Q), (P_SIZE * BOX_LEAVES) ** -0.5, 0.0068359375)
    coupling_operators = normal_values(key_of[5], (Q, 3 * Q), Q ** -0.5, 0.75, (), jnp.float32)
    coarse_weights = normal_values(key_of[6], (NC, NC), NC ** -0.5, 1.0, (), jnp.float32)
    downward_ops = normal_values(key_of[7], (8, Q, P_SIZE), Q ** -0.5, 0.75)
    conc_owner_keys = jax.random.split(jax.random.fold_in(key_of[8], 1), LEAVES // L_DEV)
    conc_owner_turns = jax.random.permutation(jax.random.fold_in(key_of[8], 3), LEAVES // L_DEV)
    conc_owner = jax.vmap(lambda own, number: routed_block(jax.random.fold_in(key_of[8], 2), own, number, L_DEV, N_LEAF, 1, CAP, 2))(conc_owner_keys, conc_owner_turns).reshape((LEAVES, 1))
    concentration = normal_values(key_of[9], (SLOTS, P_SIZE), 1.0, 6.0, ((0, 128),))
    departure = with_ends(jax.random.randint(key_of[10], (SLOTS,), 0, SLOTS_DEV), jax.random.fold_in(key_of[10], 1), 0, SLOTS_DEV - 1).astype(jnp.int32)
    departure_class = with_ends(jax.random.randint(key_of[11], (SLOTS,), 0, NCLS), jax.random.fold_in(key_of[11], 1), 0, NCLS - 1).astype(jnp.int32)
    shift_ops = normal_values(key_of[12], (NCLS, P_SIZE, P_SIZE), P_SIZE ** -0.5, 0.4375)
    eval_ops = normal_values(key_of[13], (P_SIZE, 4 * NODES), P_SIZE ** -0.5, 0.4375)
    return {"density": density, "vel_mask": vel_mask, "near_list": near_list, "near_ops": near_ops, "upward_ops": upward_ops, "coupling_operators": coupling_operators, "coarse_weights": coarse_weights, "downward_ops": downward_ops, "conc_owner": conc_owner, "concentration": concentration, "departure": departure, "departure_class": departure_class, "shift_ops": shift_ops, "eval_ops": eval_ops}


time_step = 0.5


def shifted_rows(gathered, classes, shift_ops):
    stacked_rows = jnp.einsum('rk,tkm->trm', gathered.astype(jnp.float32), shift_ops.astype(jnp.float32))
    select = (classes[None, :] == jnp.arange(shift_ops.shape[0], dtype=jnp.int32)[:, None]).astype(jnp.float32)
    return jnp.sum(stacked_rows * select[:, :, None], axis=0).astype(jnp.bfloat16)


def advect_rows(base, velocity_rows, alive_rows, eval_ops):
    eval_wide = eval_ops.astype(jnp.float32)
    value_rows = jnp.dot(base.astype(jnp.float32), eval_wide)
    nodes_count = value_rows.shape[1] // 4
    speeds = jnp.dot(velocity_rows.reshape(-1, eval_ops.shape[0]).astype(jnp.float32), eval_wide[:, :nodes_count])
    speeds = speeds.reshape(base.shape[0], 3, nodes_count)
    correction = speeds[:, 0] * value_rows[:, nodes_count:2 * nodes_count]
    correction = correction + speeds[:, 1] * value_rows[:, 2 * nodes_count:3 * nodes_count]
    correction = correction + speeds[:, 2] * value_rows[:, 3 * nodes_count:]
    return (alive_rows[:, None] * (value_rows[:, :nodes_count] - time_step * correction)).astype(jnp.bfloat16)


def reference(density, vel_mask, near_list, near_ops, upward_ops, coupling_operators, coarse_weights, downward_ops, conc_owner, concentration, departure, departure_class, shift_ops, eval_ops):
    leaves_all = density.shape[0]
    blocks = leaves_all // L_DEV
    alive = vel_mask.astype(jnp.float32)
    live_density = (density.astype(jnp.float32) * alive[:, None]).astype(jnp.bfloat16)
    parts = jnp.einsum('gop,opq->goq', live_density.reshape(-1, 8, P_SIZE).astype(jnp.float32), upward_ops.astype(jnp.float32))
    moments = jnp.sum(parts.reshape(NC, BOX_LEAVES // 8, 8, Q), axis=(1, 2))
    expanded = jnp.dot(moments, coupling_operators, precision=lax.Precision.HIGHEST)
    local_expansion = jnp.dot(coarse_weights, expanded, precision=lax.Precision.HIGHEST)
    far_all = jnp.einsum('cjq,oqp->cojp', local_expansion.reshape(NC, 3, Q), downward_ops.astype(jnp.float32), precision=lax.Precision.HIGHEST)
    flat_ops = near_ops.reshape(NEAR * P_SIZE, 3 * P_SIZE).astype(jnp.float32)

    def one_block(index):
        rows = lax.dynamic_slice_in_dim(near_list, index * L_DEV, L_DEV, 0)
        gathered = live_density[rows].reshape(L_DEV, NEAR * P_SIZE).astype(jnp.float32)
        nearby_field = jnp.dot(gathered, flat_ops)
        box_far = far_all[index // SPAN].reshape(1, 8, 3 * P_SIZE)
        far_field = jnp.broadcast_to(box_far, (L_DEV // 8, 8, 3 * P_SIZE)).reshape(L_DEV, 3 * P_SIZE)
        alive_rows = lax.dynamic_slice_in_dim(alive, index * L_DEV, L_DEV, 0)
        return ((nearby_field + far_field) * alive_rows[:, None]).astype(jnp.bfloat16)

    velocity = lax.map(one_block, jnp.arange(blocks, dtype=jnp.int32)).reshape(leaves_all, 3 * P_SIZE)
    owner = conc_owner[:, 0].reshape(blocks, L_DEV)
    onehot = (owner[:, :, None] == jnp.arange(N_LEAF, dtype=jnp.int32)[None, None, :]).astype(jnp.int32)
    rank = jnp.sum(jnp.cumsum(onehot, axis=1) * onehot, axis=2) - 1
    capacity = SLOTS_DEV // N_LEAF
    slot = owner * SLOTS_DEV + jnp.arange(blocks, dtype=jnp.int32)[:, None] * capacity + rank
    slot = slot.reshape(leaves_all).astype(jnp.int32)
    received_velocity = jnp.zeros((SLOTS, 3 * P_SIZE), jnp.bfloat16).at[slot].set(velocity)
    filled = jnp.zeros((SLOTS,), jnp.float32).at[slot].set(alive)

    def one_device(index):
        start = index * SLOTS_DEV
        conc_rows = lax.dynamic_slice_in_dim(concentration, start, SLOTS_DEV, 0)
        depart_rows = lax.dynamic_slice_in_dim(departure, start, SLOTS_DEV, 0)
        class_rows = lax.dynamic_slice_in_dim(departure_class, start, SLOTS_DEV, 0)
        base = shifted_rows(conc_rows[depart_rows], class_rows, shift_ops)
        velocity_rows = lax.dynamic_slice_in_dim(received_velocity, start, SLOTS_DEV, 0)
        alive_rows = lax.dynamic_slice_in_dim(filled, start, SLOTS_DEV, 0)
        return advect_rows(base, velocity_rows, alive_rows, eval_ops)

    advected = lax.map(one_device, jnp.arange(N_LEAF, dtype=jnp.int32)).reshape(SLOTS, NODES)
    return velocity, advected
```

```python
import jax
import jax.numpy as jnp
from jax import lax
from jax.experimental import pallas as pl
from jax.experimental.pallas import tpu as pltpu
from jax.sharding import PartitionSpec as P

SPAN = 4
TIME_STEP = 0.5
TILE = 256
LANES = 128
HIGH = lax.Precision.HIGHEST
VMEM = pl.BlockSpec(memory_space=pltpu.VMEM)


def near_kernel(
    idx_hbm, low_ref, own_ref, high_ref, ops_ref, far_ref, mask_ref,
    out_ref, pad_ref, table, picked, idx_a, idx_b, sem,
):
    positions, coefs, width = ops_ref.shape
    leaves = own_ref.shape[0]
    tiles = leaves // TILE
    half = idx_a.shape[0] // TILE
    lag = 2

    def fetch_a(k):
        return pltpu.make_async_copy(idx_hbm.at[k, pl.ds(0, half * TILE)], idx_a, sem.at[0])

    def fetch_b(k):
        return pltpu.make_async_copy(
            idx_hbm.at[k, pl.ds(half * TILE, (positions - half) * TILE)], idx_b, sem.at[1]
        )

    fetch_a(0).start()
    fetch_b(0).start()
    for part, ref in enumerate((low_ref, own_ref, high_ref)):

        def fill(s, c, ref=ref, part=part):
            x = ref[pl.ds(pl.multiple_of(s * TILE, TILE), TILE), :].astype(jnp.float32)
            start = part * 2 * leaves + s * 2 * TILE
            table[pl.ds(start, TILE, stride=2), :] = x[:, :LANES]
            table[pl.ds(start + 1, TILE, stride=2), :] = x[:, LANES:]
            return c

        lax.fori_loop(0, leaves // TILE, fill, 0)
    pad_ref[pl.ds(640, 128), :] = jnp.zeros((128, leaves), jnp.bfloat16)

    def product(t):
        first = picked[t, pl.ds(0, TILE, stride=2), :].astype(jnp.bfloat16)
        second = picked[t, pl.ds(1, TILE, stride=2), :].astype(jnp.bfloat16)
        rows = jnp.concatenate([first, second], axis=1)[:, :width]
        return lax.dot_general(
            ops_ref[t], rows, (((1,), (1,)), ((), ())), preferred_element_type=jnp.float32
        )

    def tile_step(k, c):
        later = lax.min(k + 1, tiles - 1)
        total = None
        fetch_a(0).wait()
        for t in range(positions + lag):
            if t < positions:
                if t == half:
                    fetch_a(later).start()
                    fetch_b(0).wait()
                for i in range(TILE):
                    row = idx_a[t * TILE + i] if t < half else idx_b[(t - half) * TILE + i]
                    picked[t, pl.ds(2 * i, 2), :] = table[pl.ds(pl.multiple_of(row, 2), 2), :]
            if t >= lag:
                term = product(t - lag)
                total = term if total is None else total + term
        fetch_b(later).start()
        cols = pl.ds(pl.multiple_of(k * TILE, TILE), TILE)
        far = far_ref[...]
        value = total + jnp.concatenate([far] * (TILE // LANES), axis=1)
        value = (value * mask_ref[:, cols]).astype(jnp.bfloat16)
        out_ref[:, cols] = value
        pad_ref[pl.ds(0, coefs), cols] = value
        return c

    lax.fori_loop(0, tiles, tile_step, 0)
    fetch_a(0).wait()
    fetch_b(0).wait()


def near_call(idx, low, own, high, ops, far, mask):
    positions, coefs, _ = ops.shape
    leaves = own.shape[0]
    half = (positions + 1) // 2
    return pl.pallas_call(
        near_kernel,
        out_shape=(
            jax.ShapeDtypeStruct((coefs, leaves), jnp.bfloat16),
            jax.ShapeDtypeStruct((768, leaves), jnp.bfloat16),
        ),
        in_specs=[pl.BlockSpec(memory_space=pl.ANY)] + [VMEM] * 6,
        out_specs=(VMEM, VMEM),
        scratch_shapes=[
            pltpu.VMEM((6 * leaves, LANES), jnp.float32),
            pltpu.VMEM((positions, 2 * TILE, LANES), jnp.float32),
            pltpu.SMEM((half * TILE,), jnp.int32),
            pltpu.SMEM(((positions - half) * TILE,), jnp.int32),
            pltpu.SemaphoreType.DMA((2,)),
        ],
        compiler_params=pltpu.CompilerParams(vmem_limit_bytes=40 * 2**20),
        cost_estimate=pl.CostEstimate(
            flops=2 * positions * leaves * 256 * 664, bytes_accessed=20_000_000, transcendentals=0
        ),
        name="near",
    )(idx, low, own, high, ops, far, mask)


def base_kernel(conc_ref, dep_ref, cls_ref, shift_ref, out_ref):
    slots = conc_ref.shape[1]
    rows = lax.broadcasted_iota(jnp.int32, (slots, TILE), 0)
    pick = jnp.where(rows == dep_ref[...], 1.0, 0.0).astype(jnp.bfloat16)
    got = jnp.dot(conc_ref[...], pick, preferred_element_type=jnp.float32)
    kind = cls_ref[...]
    total = None
    for c in range(shift_ref.shape[0]):
        part = jnp.where(kind == c, got, 0.0).astype(jnp.bfloat16)
        term = jnp.dot(shift_ref[c], part, preferred_element_type=jnp.float32)
        total = term if total is None else total + term
    out_ref[...] = total.astype(jnp.bfloat16)


def base_call(conc, dep, cls, shift):
    width, slots = conc.shape
    return pl.pallas_call(
        base_kernel,
        out_shape=jax.ShapeDtypeStruct((width, slots), jnp.bfloat16),
        grid=(slots // TILE,),
        in_specs=[
            pl.BlockSpec(conc.shape, lambda s: (0, 0)),
            pl.BlockSpec((1, TILE), lambda s: (0, s)),
            pl.BlockSpec((1, TILE), lambda s: (0, s)),
            pl.BlockSpec(shift.shape, lambda s: (0, 0, 0)),
        ],
        out_specs=pl.BlockSpec((width, TILE), lambda s: (0, s)),
        compiler_params=pltpu.CompilerParams(vmem_limit_bytes=24 * 2**20),
        cost_estimate=pl.CostEstimate(
            flops=2 * slots * 256 * 4096, bytes_accessed=3_000_000, transcendentals=0
        ),
        name="base",
    )(conc, dep, cls, shift)


def send_kernel(slot_ref, vel_ref, out_ref):
    rows, leaves = out_ref.shape[0], vel_ref.shape[1]
    at = lax.broadcasted_iota(jnp.int32, (rows, leaves), 0) + pl.program_id(0) * rows
    pick = jnp.where(at == slot_ref[...], 1.0, 0.0).astype(jnp.bfloat16)
    out_ref[...] = lax.dot_general(
        pick, vel_ref[...], (((1,), (1,)), ((), ())), preferred_element_type=jnp.float32
    ).astype(jnp.bfloat16)


def send_call(slot, vel, slots):
    rows = 512
    return pl.pallas_call(
        send_kernel,
        out_shape=jax.ShapeDtypeStruct((slots, vel.shape[0]), jnp.bfloat16),
        grid=(slots // rows,),
        in_specs=[
            pl.BlockSpec(slot.shape, lambda s: (0, 0)),
            pl.BlockSpec(vel.shape, lambda s: (0, 0)),
        ],
        out_specs=pl.BlockSpec((rows, vel.shape[0]), lambda s: (s, 0)),
        compiler_params=pltpu.CompilerParams(vmem_limit_bytes=24 * 2**20),
        cost_estimate=pl.CostEstimate(
            flops=2 * slots * 1024 * 768, bytes_accessed=5_000_000, transcendentals=0
        ),
        name="send",
    )(slot, vel)


def advect_kernel(base_ref, got_ref, alive_ref, eval_ref, e0_ref, e1_ref, e2_ref, out_ref):
    nodes = out_ref.shape[1]
    values = lax.dot_general(
        base_ref[...], eval_ref[...], (((0,), (0,)), ((), ())), preferred_element_type=jnp.float32
    )
    got = got_ref[...]
    correction = None
    for j, (lo, hi, ref) in enumerate(((0, 256, e0_ref), (128, 512, e1_ref), (384, 768, e2_ref))):
        speed = jnp.dot(got[:, lo:hi], ref[...], preferred_element_type=jnp.float32)
        term = speed * values[:, (j + 1) * nodes : (j + 2) * nodes]
        correction = term if correction is None else correction + term
    result = alive_ref[...] * (values[:, :nodes] - TIME_STEP * correction)
    out_ref[...] = result.astype(jnp.bfloat16)


def advect_call(base, got, alive, evals, shifted):
    width, slots = base.shape
    nodes = evals.shape[1] // 4
    return pl.pallas_call(
        advect_kernel,
        out_shape=jax.ShapeDtypeStruct((slots, nodes), jnp.bfloat16),
        grid=(slots // TILE,),
        in_specs=[
            pl.BlockSpec((width, TILE), lambda s: (0, s)),
            pl.BlockSpec((TILE, got.shape[1]), lambda s: (s, 0)),
            pl.BlockSpec((TILE, 1), lambda s: (s, 0)),
            pl.BlockSpec(evals.shape, lambda s: (0, 0)),
        ]
        + [pl.BlockSpec(e.shape, lambda s: (0, 0)) for e in shifted],
        out_specs=pl.BlockSpec((TILE, nodes), lambda s: (s, 0)),
        compiler_params=pltpu.CompilerParams(vmem_limit_bytes=24 * 2**20),
        cost_estimate=pl.CostEstimate(
            flops=2 * slots * 256 * 2304, bytes_accessed=6_000_000, transcendentals=0
        ),
        name="advect",
    )(base, got, alive, evals, *shifted)


def local(
    density,
    vel_mask,
    near_list,
    near_ops,
    upward_ops,
    coupling_operators,
    coarse_weights,
    downward_ops,
    conc_owner,
    concentration,
    departure,
    departure_class,
    shift_ops,
    eval_ops,
):
    leaves, width = density.shape
    positions = near_list.shape[1]
    devices = lax.axis_size("leaf")
    me = lax.axis_index("leaf")
    box = me // SPAN
    slots = concentration.shape[0]
    capacity = slots // devices
    nodes = eval_ops.shape[1] // 4
    forward = [(i, i + 1) for i in range(devices - 1)]
    backward = [(i + 1, i) for i in range(devices - 1)]

    alive = vel_mask.astype(jnp.float32)
    live = (density.astype(jnp.float32) * alive[:, None]).astype(jnp.bfloat16)
    own = jnp.pad(live, ((0, 0), (0, 256 - width)))
    low = lax.ppermute(own, "leaf", forward)
    high = lax.ppermute(own, "leaf", backward)

    octant = (jnp.arange(leaves, dtype=jnp.int32)[:, None] % 8) == jnp.arange(8, dtype=jnp.int32)
    sums = jnp.dot(live.T, octant.astype(jnp.bfloat16), preferred_element_type=jnp.float32)
    part = jnp.einsum("po,opq->q", sums, upward_ops.astype(jnp.float32), precision=HIGH)

    owner = conc_owner[:, 0]
    named = (jnp.arange(devices, dtype=jnp.int32)[:, None] == owner[None, :]).astype(jnp.bfloat16)
    spot = jnp.arange(leaves, dtype=jnp.int32)
    before = (spot[:, None] < spot[None, :]).astype(jnp.bfloat16)
    count = jnp.dot(named, before, preferred_element_type=jnp.float32)
    rank = jnp.sum(count * named.astype(jnp.float32), axis=0).astype(jnp.int32)
    slot = (owner * capacity + rank)[None, :]
    ranked = (rank[:, None] == jnp.arange(capacity, dtype=jnp.int32)).astype(jnp.bfloat16)
    filled = jnp.dot(
        named, ranked * vel_mask[:, None].astype(jnp.bfloat16), preferred_element_type=jnp.float32
    )
    small = jnp.concatenate(
        [
            jnp.broadcast_to(jnp.pad(part, (0, 64 - part.shape[0]))[None, :], (devices, 64)),
            filled,
            jnp.zeros((devices, 64 - capacity), jnp.float32),
        ],
        axis=1,
    ).reshape(devices, 1, 128)
    small = lax.all_to_all(small, "leaf", split_axis=0, concat_axis=0, tiled=True)
    small = small.reshape(devices, 128)

    weight_row = jnp.repeat(lax.dynamic_slice_in_dim(coarse_weights, box, 1, 0), SPAN, axis=1)
    mixed = jnp.dot(weight_row, small[:, : part.shape[0]], precision=HIGH)
    expansion = jnp.dot(mixed, coupling_operators, precision=HIGH)
    far = jnp.einsum(
        "jq,oqp->jpo",
        expansion.reshape(3, -1),
        downward_ops.astype(jnp.float32),
        precision=HIGH,
    )
    far = jnp.tile(far.reshape(3 * width, 8), (1, 16))
    alive_slots = small[:, 64 : 64 + capacity].reshape(slots, 1)

    base = base_call(
        concentration.T,
        departure[None, :],
        departure_class[None, :],
        shift_ops.transpose(0, 2, 1),
    )

    rows = (near_list.T - me * leaves + leaves) * 2
    rows = rows.reshape(positions, leaves // TILE, TILE).transpose(1, 0, 2)
    rows = rows.reshape(leaves // TILE, positions * TILE)
    velocity, padded = near_call(
        rows, low, own, high, near_ops.transpose(0, 2, 1), far, alive[None, :]
    )
    send = send_call(slot, padded, slots)
    got = lax.all_to_all(
        send.reshape(devices, capacity, -1), "leaf", split_axis=0, concat_axis=0, tiled=True
    )
    first = eval_ops[:, :nodes]
    shifted = (
        jnp.pad(first, ((0, 256 - width), (0, 0))),
        jnp.pad(first, ((width - 128, 512 - 2 * width), (0, 0))),
        jnp.pad(first, ((2 * width - 384, 768 - 3 * width), (0, 0))),
    )
    advected = advect_call(base, got.reshape(slots, -1), alive_slots, eval_ops, shifted)
    return velocity.T, advected


def solution(mesh):
    placed = (
        P("leaf", None),
        P("leaf"),
        P("leaf", None),
        P(),
        P(),
        P(),
        P(),
        P(),
        P("leaf", None),
        P("leaf", None),
        P("leaf"),
        P("leaf"),
        P(),
        P(),
    )
    return jax.shard_map(
        local,
        mesh=mesh,
        in_specs=placed,
        out_specs=(P("leaf", None), P("leaf", None)),
        check_vma=False,
    )
```

```python
import jax
import jax.numpy as jnp
from jax import lax
from jax.experimental import pallas as pl
from jax.experimental.pallas import tpu as pltpu
from jax.sharding import PartitionSpec as P

SPAN = 4
TIME_STEP = 0.5
TILE = 256
LANES = 128
CAP = 16
NEAR_TILE = 512
NEAR_GROUP = 13
HIGH = lax.Precision.HIGHEST
VMEM = pl.BlockSpec(memory_space=pltpu.VMEM)


def live_kernel(density_ref, mask_ref, out_ref):
    width, leaves = density_ref.shape
    x = density_ref[...].astype(jnp.float32) * mask_ref[...].astype(jnp.float32)
    x = jnp.concatenate([x, jnp.zeros((256 - width, leaves), jnp.float32)], axis=0)
    out_ref[...] = x.T.astype(jnp.bfloat16)


def live_call(density, mask):
    return pl.pallas_call(
        live_kernel,
        out_shape=jax.ShapeDtypeStruct((density.shape[1], 256), jnp.bfloat16),
        in_specs=[VMEM, VMEM],
        out_specs=VMEM,
        compiler_params=pltpu.CompilerParams(vmem_limit_bytes=62 * 2**20),
        name="live",
    )(density, mask)


def near_kernel(
    idx_hbm, low_hbm, own_hbm, high_hbm, ops_hbm, out_hbm,
    table, picked, parts, ops, sums, idx_a, idx_b, idx_sem, part_sem, ops_sem, out_sem,
):
    positions, _, width = ops.shape
    leaves = parts.shape[1]
    group = picked.shape[0]
    groups = (positions - 1) // group
    center = group
    steps = leaves // NEAR_TILE * groups
    half = idx_a.shape[0] // NEAR_TILE

    def fetch_a(k):
        return pltpu.make_async_copy(
            idx_hbm.at[k, pl.ds(0, half * NEAR_TILE)], idx_a, idx_sem.at[0]
        )

    def fetch_b(k):
        return pltpu.make_async_copy(
            idx_hbm.at[k, pl.ds(half * NEAR_TILE, (group - half) * NEAR_TILE)],
            idx_b,
            idx_sem.at[1],
        )

    def fetch_ops(k):
        rows = pl.ds(k * (group + 1), group)
        return pltpu.make_async_copy(ops_hbm.at[rows], ops.at[rows], ops_sem.at[k])

    middle = pltpu.make_async_copy(ops_hbm.at[center], ops.at[center], ops_sem.at[groups])

    def contract_rows(position, rows):
        return lax.dot_general(
            ops[position], rows, (((1,), (1,)), ((), ())), preferred_element_type=jnp.float32
        )

    order = ((1, own_hbm), (0, low_hbm), (2, high_hbm))
    copies = [pltpu.make_async_copy(ref, parts.at[p], part_sem.at[p]) for p, ref in order]
    copies[0].start()
    middle.start()
    fetch_a(0).start()
    fetch_b(0).start()
    for copy in copies[1:]:
        copy.start()
    for k in range(groups):
        fetch_ops(k).start()
    picked[group - 1] = jnp.zeros((2 * NEAR_TILE, LANES), jnp.float32)
    for (part, _), copy in zip(order, copies):
        copy.wait()

        def fill(s, c, part=part):
            x = parts[part, pl.ds(pl.multiple_of(s * TILE, TILE), TILE), :].astype(jnp.float32)
            start = part * 2 * leaves + s * 2 * TILE
            table[pl.ds(start, TILE, stride=2), :] = x[:, :LANES]
            table[pl.ds(start + 1, TILE, stride=2), :] = x[:, LANES:]
            return c

        lax.fori_loop(0, leaves // TILE, fill, 0)
        if part == 1:
            middle.wait()
            for tile in range(leaves // NEAR_TILE):
                rows = parts[1, pl.ds(tile * NEAR_TILE, NEAR_TILE), :][:, :width]
                sums[tile] = contract_rows(center, rows)

    def product(t, position):
        first = picked[t, pl.ds(0, NEAR_TILE, stride=2), :].astype(jnp.bfloat16)
        second = picked[t, pl.ds(1, NEAR_TILE, stride=2), :].astype(jnp.bfloat16)
        return contract_rows(position, jnp.concatenate([first, second], axis=1)[:, :width])

    def store(tile):
        cols = pl.ds(pl.multiple_of(tile * NEAR_TILE, NEAR_TILE), NEAR_TILE)
        return pltpu.make_async_copy(sums.at[tile], out_hbm.at[:, cols], out_sem.at[tile])

    def step(s, c):
        tile = lax.div(s, groups)
        g = s - tile * groups
        last = lax.max(s - 1, 0)
        last_tile = lax.div(last, groups)
        last_position = (last - last_tile * groups) * (group + 1) + group - 1
        later = lax.min(s + 1, steps - 1)

        @pl.when(s < groups)
        def _():
            fetch_ops(s).wait()

        @pl.when((g == 1) & (tile > 0))
        def _():
            store(tile - 1).start()

        fetch_a(0).wait()
        total = None
        for t in range(group):
            if t == half:
                fetch_a(later).start()
                fetch_b(0).wait()
            for i in range(NEAR_TILE):
                at = t * NEAR_TILE + i
                row = idx_a[at] if t < half else idx_b[at - half * NEAR_TILE]
                picked[t, pl.ds(2 * i, 2), :] = table[pl.ds(pl.multiple_of(row, 2), 2), :]
            if t == 0:
                sums[last_tile] += product(group - 1, last_position)
            else:
                term = product(t - 1, g * (group + 1) + t - 1)
                total = term if total is None else total + term
        fetch_b(later).start()
        sums[tile] += total
        return c

    tiles = leaves // NEAR_TILE
    lax.fori_loop(0, steps, step, 0)
    sums[tiles - 1] += product(group - 1, positions - 1)
    store(tiles - 1).start()
    for tile in range(tiles):
        store(tile).wait()
    fetch_a(0).wait()
    fetch_b(0).wait()


def near_call(idx, low, own, high, ops):
    positions, coefs, width = ops.shape
    leaves = own.shape[0]
    half = (NEAR_GROUP + 1) // 2
    anywhere = pl.BlockSpec(memory_space=pl.ANY)
    return pl.pallas_call(
        near_kernel,
        out_shape=jax.ShapeDtypeStruct((coefs, leaves), jnp.float32),
        in_specs=[anywhere] * 5,
        out_specs=anywhere,
        scratch_shapes=[
            pltpu.VMEM((6 * leaves, LANES), jnp.float32),
            pltpu.VMEM((NEAR_GROUP, 2 * NEAR_TILE, LANES), jnp.float32),
            pltpu.VMEM((3,) + own.shape, jnp.bfloat16),
            pltpu.VMEM(ops.shape, jnp.bfloat16),
            pltpu.VMEM((leaves // NEAR_TILE, coefs, NEAR_TILE), jnp.float32),
            pltpu.SMEM((half * NEAR_TILE,), jnp.int32),
            pltpu.SMEM(((NEAR_GROUP - half) * NEAR_TILE,), jnp.int32),
            pltpu.SemaphoreType.DMA((2,)),
            pltpu.SemaphoreType.DMA((3,)),
            pltpu.SemaphoreType.DMA(((positions - 1) // NEAR_GROUP + 1,)),
            pltpu.SemaphoreType.DMA((leaves // NEAR_TILE,)),
        ],
        compiler_params=pltpu.CompilerParams(
            vmem_limit_bytes=60 * 2**20,
        ),
        cost_estimate=pl.CostEstimate(
            flops=2 * positions * leaves * 256 * 1024, bytes_accessed=20_000_000, transcendentals=0
        ),
        name="near",
    )(idx, low, own, high, ops)


def base_kernel(conc_ref, dep_ref, cls_ref, shift_ref, eval_ref, out_ref):
    slots = conc_ref.shape[1]
    rows = lax.broadcasted_iota(jnp.int32, (slots, TILE), 0)
    pick = jnp.where(rows == dep_ref[...], 1.0, 0.0).astype(jnp.bfloat16)
    got = jnp.dot(conc_ref[...], pick, preferred_element_type=jnp.float32)
    kind = cls_ref[...]
    total = None
    for c in range(shift_ref.shape[0]):
        part = jnp.where(kind == c, got, 0.0).astype(jnp.bfloat16)
        term = jnp.dot(shift_ref[c], part, preferred_element_type=jnp.float32)
        total = term if total is None else total + term
    base = total.astype(jnp.bfloat16)
    out_ref[...] = lax.dot_general(
        base, eval_ref[...], (((0,), (0,)), ((), ())), preferred_element_type=jnp.float32
    ).astype(jnp.bfloat16)


def base_call(conc, dep, cls, shift, evals):
    width, slots = conc.shape
    return pl.pallas_call(
        base_kernel,
        out_shape=jax.ShapeDtypeStruct((slots, evals.shape[1]), jnp.bfloat16),
        grid=(slots // TILE,),
        in_specs=[
            pl.BlockSpec(conc.shape, lambda s: (0, 0)),
            pl.BlockSpec((1, TILE), lambda s: (0, s)),
            pl.BlockSpec((1, TILE), lambda s: (0, s)),
            pl.BlockSpec(shift.shape, lambda s: (0, 0, 0)),
            pl.BlockSpec(evals.shape, lambda s: (0, 0)),
        ],
        out_specs=pl.BlockSpec((TILE, evals.shape[1]), lambda s: (s, 0)),
        compiler_params=pltpu.CompilerParams(vmem_limit_bytes=62 * 2**20),
        cost_estimate=pl.CostEstimate(
            flops=2 * slots * 256 * 4096, bytes_accessed=3_000_000, transcendentals=0
        ),
        name="base",
    )(conc, dep, cls, shift, evals)


def send_kernel(slot_ref, sum_ref, mask_ref, parts_ref, out_ref, value, extra):
    owners, rows, _ = out_ref.shape
    coefs, leaves = sum_ref.shape
    whole = coefs // LANES * LANES

    @pl.when(pl.program_id(0) == 0)
    def _():
        mask = mask_ref[...]
        value[...] = (sum_ref[...] * mask).astype(jnp.bfloat16)
        kind = lax.broadcasted_iota(jnp.int32, (8, leaves), 0)
        spot = lax.broadcasted_iota(jnp.int32, (8, leaves), 1)
        octant = jnp.where((spot & 7) == kind, mask, 0.0).astype(jnp.bfloat16)
        extra[...] = jnp.zeros_like(extra)
        for b in range(2):
            extra[b, pl.ds(64 * b, coefs - whole), :] = value[pl.ds(whole, coefs - whole), :]
            extra[b, pl.ds(64 * b + 32, 8), :] = octant

    def pick(count, place):
        row = lax.broadcasted_iota(jnp.int32, (count, leaves), 0)
        at = place(row) + pl.program_id(0) * (owners * CAP)
        return jnp.where(at == slot_ref[...], 1.0, 0.0).astype(jnp.bfloat16)

    contract = (((1,), (1,)), ((), ()))
    main = lax.dot_general(
        pick(owners * CAP, lambda r: r), value[pl.ds(0, whole), :], contract,
        preferred_element_type=jnp.float32,
    ).astype(jnp.bfloat16)
    for q in range(whole // LANES):
        out_ref[:, q * CAP : (q + 1) * CAP, :] = main[:, q * LANES : (q + 1) * LANES].reshape(
            owners, CAP, LANES
        )
    rest = None
    for b in range(2):
        term = lax.dot_general(
            pick(owners * 8, lambda r: r + (r & ~7) + 8 * b), extra[b], contract,
            preferred_element_type=jnp.float32,
        )
        rest = term if rest is None else rest + term
    rest = rest.reshape(owners, 8, LANES) + parts_ref[...][None]
    out_ref[:, whole // LANES * CAP :, :] = rest.astype(jnp.bfloat16)


def send_call(slot, total, mask, parts, devices):
    coefs, leaves = total.shape
    owners = 64
    rows = coefs // LANES * CAP + 8
    whole = lambda x: pl.BlockSpec(x.shape, lambda s: (0, 0))
    return pl.pallas_call(
        send_kernel,
        out_shape=jax.ShapeDtypeStruct((devices, rows, LANES), jnp.bfloat16),
        grid=(devices // owners,),
        in_specs=[whole(x) for x in (slot, total, mask, parts)],
        out_specs=pl.BlockSpec((owners, rows, LANES), lambda s: (s, 0, 0)),
        scratch_shapes=[
            pltpu.VMEM((coefs, leaves), jnp.bfloat16),
            pltpu.VMEM((2, LANES, leaves), jnp.bfloat16),
        ],
        compiler_params=pltpu.CompilerParams(vmem_limit_bytes=60 * 2**20),
        cost_estimate=pl.CostEstimate(
            flops=2 * devices * CAP * 1024 * 768, bytes_accessed=8_000_000, transcendentals=0
        ),
        name="send",
    )(slot, total, mask, parts)


def split(x):
    high = x.astype(jnp.bfloat16)
    rest = x - high.astype(jnp.float32)
    middle = rest.astype(jnp.bfloat16)
    return high, middle, (rest - middle.astype(jnp.float32)).astype(jnp.bfloat16)


def advect_kernel(
    box_ref, values_ref, got_ref, parts_ref, first_ref, weights_ref, couple_ref, node_ref,
    down_ref, spread_ref, sum_ref, mask_ref, out_ref, vel_ref, table, far,
):
    nodes = out_ref.shape[1]
    owners = got_ref.shape[0]
    boxes = weights_ref.shape[0] // 6
    step = pl.program_id(0)

    @pl.when(step == 0)
    def _():
        sent = parts_ref[...].reshape(parts_ref.shape[0] * 8, LANES)
        mixed = jnp.dot(weights_ref[...], sent, preferred_element_type=jnp.float32)
        mixed = mixed.reshape(3, 2, boxes, LANES)
        mixed = mixed[0] + mixed[1] + mixed[2]
        mixed = jnp.concatenate([mixed[0], mixed[1]], axis=1)
        expansion = jnp.dot(
            mixed, couple_ref[...], precision=HIGH, preferred_element_type=jnp.float32
        )
        stacked = jnp.concatenate(
            [expansion[:, j * LANES : (j + 1) * LANES] for j in range(3)], axis=0
        )
        boxed = jnp.dot(
            stacked.astype(jnp.bfloat16), node_ref[...], preferred_element_type=jnp.float32
        ).astype(jnp.bfloat16)
        for j in range(3):
            for o in range(8):
                table[j, o * boxes : (o + 1) * boxes, :] = boxed[
                    j * boxes : (j + 1) * boxes, o * nodes : (o + 1) * nodes
                ]
        row = lax.broadcasted_iota(jnp.int32, (boxes, 3 * LANES), 0)
        mine = jnp.sum(jnp.where(row == box_ref[0], expansion, 0.0), axis=0, keepdims=True)
        for j in range(3):
            own = jnp.broadcast_to(mine[:, j * LANES : (j + 1) * LANES], (8, LANES))
            kind = lax.broadcasted_iota(jnp.int32, (8, 256), 0)
            field = jnp.zeros((8, 256), jnp.float32)
            for piece in split(own):
                wide = jnp.dot(piece, down_ref[...], preferred_element_type=jnp.float32)
                for o in range(8):
                    field = field + jnp.where(kind == o, wide[:, o * 256 : (o + 1) * 256], 0.0)
            far[j] = jnp.concatenate([field] * 16, axis=0).T

    width = vel_ref.shape[0] // 3
    for j in range(3):
        rows = pl.ds(j * width, width)
        shade = jnp.concatenate([far[j, pl.ds(0, width), :]] * (vel_ref.shape[1] // LANES), axis=1)
        vel_ref[rows, :] = ((sum_ref[rows, :] + shade) * mask_ref[...]).astype(jnp.bfloat16)

    tiles = [
        got_ref[:, q * CAP : (q + 1) * CAP, :].reshape(owners * CAP, LANES) for q in range(5)
    ]
    last = got_ref[:, 5 * CAP :, :].reshape(owners * 8, LANES)

    def times(left, start):
        right = first_ref[pl.ds(start, left.shape[1]), :]
        return jnp.dot(left, right, preferred_element_type=jnp.float32)

    def joined(halves):
        halves = [half.reshape(owners, 8, nodes) for half in halves]
        return jnp.concatenate(halves, axis=1).reshape(owners * CAP, nodes)

    octant = joined(
        [jnp.dot(last, spread_ref[b], preferred_element_type=jnp.float32) for b in range(2)]
    )
    lane = lax.broadcasted_iota(jnp.int32, octant.shape, 1) & (boxes - 1)
    place = lax.broadcasted_iota(jnp.int32, octant.shape, 0)
    place = lax.shift_right_logical(place, 6) + step * (owners // SPAN)
    choice = jnp.where(lane == place, octant, 0.0).astype(jnp.bfloat16)
    speeds = (
        times(jnp.concatenate(tiles[0:2], axis=1), 0),
        times(jnp.concatenate(tiles[1:4], axis=1), 256),
        times(jnp.concatenate(tiles[3:5], axis=1), 640)
        + joined([times(last, 896 + LANES * b) for b in range(2)]),
    )
    correction = None
    for j, speed in enumerate(speeds):
        speed = speed + jnp.dot(choice, table[j], preferred_element_type=jnp.float32)
        term = speed * values_ref[:, (j + 1) * nodes : (j + 2) * nodes].astype(jnp.float32)
        correction = term if correction is None else correction + term
    value = values_ref[:, :nodes].astype(jnp.float32)
    alive = jnp.max(octant, axis=1, keepdims=True)
    out_ref[...] = (alive * (value - TIME_STEP * correction)).astype(jnp.bfloat16)


def advect_call(box, values, got, first, weights, couple, node, down, spread, total, mask):
    slots = values.shape[0]
    nodes = values.shape[1] // 4
    coefs, leaves = total.shape
    rows = 512
    steps = slots // rows
    same = lambda x: pl.BlockSpec(x.shape, lambda s, b: (0,) * x.ndim)
    return pl.pallas_call(
        advect_kernel,
        out_shape=(
            jax.ShapeDtypeStruct((slots, nodes), jnp.bfloat16),
            jax.ShapeDtypeStruct((coefs, leaves), jnp.bfloat16),
        ),
        grid_spec=pltpu.PrefetchScalarGridSpec(
            num_scalar_prefetch=1,
            grid=(steps,),
            in_specs=[
                pl.BlockSpec((rows, values.shape[1]), lambda s, b: (s, 0)),
                pl.BlockSpec((rows // CAP,) + got.shape[1:], lambda s, b: (s, 0, 0)),
                pl.BlockSpec((got.shape[0], 8, LANES), lambda s, b: (0, 10, 0)),
            ]
            + [same(x) for x in (first, weights, couple, node, down, spread)]
            + [
                pl.BlockSpec((coefs, leaves // steps), lambda s, b: (0, s)),
                pl.BlockSpec((1, leaves // steps), lambda s, b: (0, s)),
            ],
            out_specs=(
                pl.BlockSpec((rows, nodes), lambda s, b: (s, 0)),
                pl.BlockSpec((coefs, leaves // steps), lambda s, b: (0, s)),
            ),
            scratch_shapes=[
                pltpu.VMEM((3, 256, nodes), jnp.bfloat16),
                pltpu.VMEM((3, 256, LANES), jnp.float32),
            ],
        ),
        compiler_params=pltpu.CompilerParams(vmem_limit_bytes=62 * 2**20),
        cost_estimate=pl.CostEstimate(
            flops=2 * slots * 256 * 2304, bytes_accessed=14_000_000, transcendentals=0
        ),
        name="advect",
    )(box, values, got, got, first, weights, couple, node, down, spread, total, mask)


def local(
    density,
    vel_mask,
    near_list,
    near_ops,
    upward_ops,
    coupling_operators,
    coarse_weights,
    downward_ops,
    conc_owner,
    concentration,
    departure,
    departure_class,
    shift_ops,
    eval_ops,
):
    leaves, width = density.shape
    positions = near_list.shape[1]
    devices = lax.axis_size("leaf")
    me = lax.axis_index("leaf")
    box = me // SPAN
    slots = concentration.shape[0]
    capacity = slots // devices
    nodes = eval_ops.shape[1] // 4
    forward = [(i, i + 1) for i in range(devices - 1)]
    backward = [(i + 1, i) for i in range(devices - 1)]

    alive = vel_mask.astype(jnp.float32)
    own = live_call(density.T, vel_mask[None, :])
    low = lax.ppermute(own, "leaf", forward)
    high = lax.ppermute(own, "leaf", backward)

    octant = (jnp.arange(leaves, dtype=jnp.int32)[:, None] % 8) == jnp.arange(8, dtype=jnp.int32)
    sums = jnp.dot(own.T, octant.astype(jnp.bfloat16), preferred_element_type=jnp.float32)[:width]
    part = jnp.einsum("po,opq->q", sums, upward_ops.astype(jnp.float32), precision=HIGH)

    owner = conc_owner[:, 0]
    named = (jnp.arange(devices, dtype=jnp.int32)[:, None] == owner[None, :]).astype(jnp.bfloat16)
    spot = jnp.arange(leaves, dtype=jnp.int32)
    before = (spot[:, None] < spot[None, :]).astype(jnp.bfloat16)
    count = jnp.dot(named, before, preferred_element_type=jnp.float32)
    rank = jnp.sum(count * named.astype(jnp.float32), axis=0).astype(jnp.int32)
    slot = (owner * capacity + rank)[None, :]
    high_part = lax.reduce_precision(part, 8, 7)
    middle_part = lax.reduce_precision(part - high_part, 8, 7)
    pieces = jnp.stack([high_part, middle_part, part - high_part - middle_part])
    none = lambda n: jnp.zeros((3, n), jnp.float32)
    even = jnp.concatenate([none(40), pieces[:, :24], none(40), pieces[:, 24:48]], axis=1)
    odd = jnp.concatenate([none(40), pieces[:, 48:], none(80)], axis=1)
    parts = jnp.pad(jnp.stack([even, odd], axis=1).reshape(6, LANES), ((0, 2), (0, 0)))

    rows = (near_list.T - me * leaves + leaves) * 2
    groups = (positions - 1) // NEAR_GROUP
    rows = jnp.concatenate([rows[:NEAR_GROUP], rows[NEAR_GROUP + 1 :]], axis=0)
    rows = rows.reshape(groups, NEAR_GROUP, leaves // NEAR_TILE, NEAR_TILE)
    rows = rows.transpose(2, 0, 1, 3).reshape(-1, NEAR_GROUP * NEAR_TILE)
    total = near_call(rows, low, own, high, near_ops.transpose(0, 2, 1))
    send = send_call(slot, total, alive[None, :], parts, devices)
    eval_ops, shift_ops, coarse_weights, coupling_operators, downward_ops, send = (
        lax.optimization_barrier(
            (eval_ops, shift_ops, coarse_weights, coupling_operators, downward_ops, send)
        )
    )
    got = lax.all_to_all(send, "leaf", split_axis=0, concat_axis=0, tiled=True)
    values = base_call(
        concentration.T,
        departure[None, :],
        departure_class[None, :],
        shift_ops.transpose(0, 2, 1),
        eval_ops,
    )

    one = eval_ops[:, :nodes]
    tail = 3 * width - 640
    starts = ((0, 0, width), (256 + width - 128, 0, width), (640 + 2 * width - 384, 0, width - tail))
    starts = starts + ((896, width - tail, tail), (896 + LANES + 64, width - tail, tail))
    target = jnp.arange(1152, dtype=jnp.int32)[:, None]
    source = jnp.arange(width, dtype=jnp.int32)[None, :]
    place = jnp.zeros((1152, width), bool)
    for at, origin, count in starts:
        inside = (target >= at) & (target < at + count)
        place = place | (inside & (target - at + origin == source))
    first = jnp.dot(place.astype(jnp.bfloat16), one, preferred_element_type=jnp.float32)
    first = first.astype(jnp.bfloat16)
    boxes = coarse_weights.shape[0]
    spot = jnp.arange(8 * devices, dtype=jnp.int32)
    wide = jnp.repeat(coarse_weights, 8 * SPAN, axis=1)
    wide_high = lax.reduce_precision(wide, 8, 7)
    wide_middle = lax.reduce_precision(wide - wide_high, 8, 7)
    wide = jnp.stack([wide_high, wide_middle, wide - wide_high - wide_middle])[:, None]
    parity = jnp.arange(2, dtype=jnp.int32)[None, :, None, None]
    used = (spot % 2 == parity) & (spot % 8 < 6)
    weights = jnp.where(used, wide, 0.0).reshape(6 * boxes, -1).astype(jnp.bfloat16)
    couple = jnp.pad(coupling_operators.reshape(-1, 3, 56), ((0, 0), (0, 0), (0, LANES - 56)))
    couple = couple.reshape(-1, 3 * LANES)
    blank = lambda n: jnp.zeros((n, 3 * LANES), jnp.float32)
    couple = jnp.concatenate(
        [blank(40), couple[:24], blank(40), couple[24:48], blank(40), couple[48:], blank(80)]
    )
    node = jnp.einsum(
        "oqp,pn->qon", downward_ops, one, preferred_element_type=jnp.float32
    ).reshape(56, 8 * nodes)
    node = jnp.pad(node, ((0, LANES - 56), (0, 0))).astype(jnp.bfloat16)
    down = jnp.pad(downward_ops.transpose(1, 0, 2), ((0, LANES - 56), (0, 0), (0, 256 - width)))
    down = down.reshape(LANES, 8 * 256)
    lane = jnp.arange(LANES, dtype=jnp.int32)[:, None]
    column = jnp.arange(8 * boxes, dtype=jnp.int32)[None, :] // boxes
    spread = jnp.stack([(lane == 32 + 64 * b + column) for b in range(2)]).astype(jnp.bfloat16)
    advected, velocity = advect_call(
        box[None].astype(jnp.int32), values, got, first, weights, couple, node, down, spread,
        total, alive[None, :],
    )
    return velocity.T, advected


def solution(mesh):
    placed = (
        P("leaf", None),
        P("leaf"),
        P("leaf", None),
        P(),
        P(),
        P(),
        P(),
        P(),
        P("leaf", None),
        P("leaf", None),
        P("leaf"),
        P("leaf"),
        P(),
        P(),
    )
    return jax.shard_map(
        local,
        mesh=mesh,
        in_specs=placed,
        out_specs=(P("leaf", None), P("leaf", None)),
        check_vma=False,
    )
```

```python
import jax
import jax.numpy as jnp
from jax import lax
from jax.experimental import pallas as pl
from jax.experimental.pallas import tpu as pltpu
from jax.sharding import PartitionSpec as P

SPAN = 4
TIME_STEP = 0.5
TILE = 256
LANES = 128
CAP = 16
NEAR_TILE = 512
NEAR_GROUP = 13
HIGH = lax.Precision.HIGHEST
VMEM = pl.BlockSpec(memory_space=pltpu.VMEM)


def live_kernel(density_ref, mask_ref, out_ref):
    width, leaves = density_ref.shape
    x = density_ref[...].astype(jnp.float32) * mask_ref[...].astype(jnp.float32)
    x = jnp.concatenate([x, jnp.zeros((256 - width, leaves), jnp.float32)], axis=0)
    out_ref[...] = x.T.astype(jnp.bfloat16)


def live_call(density, mask):
    return pl.pallas_call(
        live_kernel,
        out_shape=jax.ShapeDtypeStruct((density.shape[1], 256), jnp.bfloat16),
        in_specs=[VMEM, VMEM],
        out_specs=VMEM,
        compiler_params=pltpu.CompilerParams(vmem_limit_bytes=62 * 2**20),
        name="live",
    )(density, mask)


def near_kernel(
    idx_hbm, low_hbm, own_hbm, high_hbm, ops_hbm, out_hbm,
    table, picked, parts, ops, sums, idx_a, idx_b, idx_sem, part_sem, ops_sem, out_sem,
):
    positions, _, width = ops.shape
    leaves = parts.shape[1]
    group = picked.shape[0]
    groups = (positions - 1) // group
    center = group
    steps = leaves // NEAR_TILE * groups
    half = idx_a.shape[0] // NEAR_TILE

    def fetch_a(k):
        return pltpu.make_async_copy(
            idx_hbm.at[k, pl.ds(0, half * NEAR_TILE)], idx_a, idx_sem.at[0]
        )

    def fetch_b(k):
        return pltpu.make_async_copy(
            idx_hbm.at[k, pl.ds(half * NEAR_TILE, (group - half) * NEAR_TILE)],
            idx_b,
            idx_sem.at[1],
        )

    def fetch_ops(k):
        rows = pl.ds(k * (group + 1), group)
        return pltpu.make_async_copy(ops_hbm.at[rows], ops.at[rows], ops_sem.at[k])

    middle = pltpu.make_async_copy(ops_hbm.at[center], ops.at[center], ops_sem.at[groups])

    def contract_rows(position, rows):
        return lax.dot_general(
            ops[position], rows, (((1,), (1,)), ((), ())), preferred_element_type=jnp.float32
        )

    order = ((1, own_hbm), (0, low_hbm), (2, high_hbm))
    copies = [pltpu.make_async_copy(ref, parts.at[p], part_sem.at[p]) for p, ref in order]
    copies[0].start()
    middle.start()
    fetch_a(0).start()
    fetch_b(0).start()
    for copy in copies[1:]:
        copy.start()
    for k in range(groups):
        fetch_ops(k).start()
    picked[group - 1] = jnp.zeros((2 * NEAR_TILE, LANES), jnp.float32)
    for (part, _), copy in zip(order, copies):
        copy.wait()

        def fill(s, c, part=part):
            x = parts[part, pl.ds(pl.multiple_of(s * TILE, TILE), TILE), :].astype(jnp.float32)
            start = part * 2 * leaves + s * 2 * TILE
            table[pl.ds(start, TILE, stride=2), :] = x[:, :LANES]
            table[pl.ds(start + 1, TILE, stride=2), :] = x[:, LANES:]
            return c

        lax.fori_loop(0, leaves // TILE, fill, 0)
        if part == 1:
            middle.wait()
            for tile in range(leaves // NEAR_TILE):
                rows = parts[1, pl.ds(tile * NEAR_TILE, NEAR_TILE), :][:, :width]
                sums[tile] = contract_rows(center, rows)

    def product(t, position):
        first = picked[t, pl.ds(0, NEAR_TILE, stride=2), :].astype(jnp.bfloat16)
        second = picked[t, pl.ds(1, NEAR_TILE, stride=2), :].astype(jnp.bfloat16)
        return contract_rows(position, jnp.concatenate([first, second], axis=1)[:, :width])

    def store(tile):
        cols = pl.ds(pl.multiple_of(tile * NEAR_TILE, NEAR_TILE), NEAR_TILE)
        return pltpu.make_async_copy(sums.at[tile], out_hbm.at[:, cols], out_sem.at[tile])

    def step(s, c):
        tile = lax.div(s, groups)
        g = s - tile * groups
        last = lax.max(s - 1, 0)
        last_tile = lax.div(last, groups)
        last_position = (last - last_tile * groups) * (group + 1) + group - 1
        later = lax.min(s + 1, steps - 1)

        @pl.when(s < groups)
        def _():
            fetch_ops(s).wait()

        @pl.when((g == 1) & (tile > 0))
        def _():
            store(tile - 1).start()

        fetch_a(0).wait()
        total = None
        for t in range(group):
            if t == half:
                fetch_a(later).start()
                fetch_b(0).wait()
            for i in range(NEAR_TILE):
                at = t * NEAR_TILE + i
                row = idx_a[at] if t < half else idx_b[at - half * NEAR_TILE]
                picked[t, pl.ds(2 * i, 2), :] = table[pl.ds(pl.multiple_of(row, 2), 2), :]
            if t == 0:
                sums[last_tile] += product(group - 1, last_position)
            else:
                term = product(t - 1, g * (group + 1) + t - 1)
                total = term if total is None else total + term
        fetch_b(later).start()
        sums[tile] += total
        return c

    tiles = leaves // NEAR_TILE
    lax.fori_loop(0, steps, step, 0)
    sums[tiles - 1] += product(group - 1, positions - 1)
    store(tiles - 1).start()
    for tile in range(tiles):
        store(tile).wait()
    fetch_a(0).wait()
    fetch_b(0).wait()


def near_call(idx, low, own, high, ops):
    positions, coefs, width = ops.shape
    leaves = own.shape[0]
    half = (NEAR_GROUP + 1) // 2
    anywhere = pl.BlockSpec(memory_space=pl.ANY)
    return pl.pallas_call(
        near_kernel,
        out_shape=jax.ShapeDtypeStruct((coefs, leaves), jnp.float32),
        in_specs=[anywhere] * 5,
        out_specs=anywhere,
        scratch_shapes=[
            pltpu.VMEM((6 * leaves, LANES), jnp.float32),
            pltpu.VMEM((NEAR_GROUP, 2 * NEAR_TILE, LANES), jnp.float32),
            pltpu.VMEM((3,) + own.shape, jnp.bfloat16),
            pltpu.VMEM(ops.shape, jnp.bfloat16),
            pltpu.VMEM((leaves // NEAR_TILE, coefs, NEAR_TILE), jnp.float32),
            pltpu.SMEM((half * NEAR_TILE,), jnp.int32),
            pltpu.SMEM(((NEAR_GROUP - half) * NEAR_TILE,), jnp.int32),
            pltpu.SemaphoreType.DMA((2,)),
            pltpu.SemaphoreType.DMA((3,)),
            pltpu.SemaphoreType.DMA(((positions - 1) // NEAR_GROUP + 1,)),
            pltpu.SemaphoreType.DMA((leaves // NEAR_TILE,)),
        ],
        compiler_params=pltpu.CompilerParams(
            vmem_limit_bytes=60 * 2**20,
        ),
        cost_estimate=pl.CostEstimate(
            flops=2 * positions * leaves * 256 * 1024, bytes_accessed=20_000_000, transcendentals=0
        ),
        name="near",
    )(idx, low, own, high, ops)


def base_kernel(conc_ref, dep_ref, cls_ref, shift_ref, eval_ref, out_ref):
    slots = conc_ref.shape[1]
    rows = lax.broadcasted_iota(jnp.int32, (slots, TILE), 0)
    pick = jnp.where(rows == dep_ref[...], 1.0, 0.0).astype(jnp.bfloat16)
    got = jnp.dot(conc_ref[...], pick, preferred_element_type=jnp.float32)
    kind = cls_ref[...]
    total = None
    for c in range(shift_ref.shape[0]):
        part = jnp.where(kind == c, got, 0.0).astype(jnp.bfloat16)
        term = jnp.dot(shift_ref[c], part, preferred_element_type=jnp.float32)
        total = term if total is None else total + term
    base = total.astype(jnp.bfloat16)
    out_ref[...] = lax.dot_general(
        base, eval_ref[...], (((0,), (0,)), ((), ())), preferred_element_type=jnp.float32
    ).astype(jnp.bfloat16)


def base_call(conc, dep, cls, shift, evals):
    width, slots = conc.shape
    return pl.pallas_call(
        base_kernel,
        out_shape=jax.ShapeDtypeStruct((slots, evals.shape[1]), jnp.bfloat16),
        grid=(slots // TILE,),
        in_specs=[
            pl.BlockSpec(conc.shape, lambda s: (0, 0)),
            pl.BlockSpec((1, TILE), lambda s: (0, s)),
            pl.BlockSpec((1, TILE), lambda s: (0, s)),
            pl.BlockSpec(shift.shape, lambda s: (0, 0, 0)),
            pl.BlockSpec(evals.shape, lambda s: (0, 0)),
        ],
        out_specs=pl.BlockSpec((TILE, evals.shape[1]), lambda s: (s, 0)),
        compiler_params=pltpu.CompilerParams(vmem_limit_bytes=62 * 2**20),
        cost_estimate=pl.CostEstimate(
            flops=2 * slots * 256 * 4096, bytes_accessed=3_000_000, transcendentals=0
        ),
        name="base",
    )(conc, dep, cls, shift, evals)


def send_kernel(slot_ref, sum_ref, mask_ref, parts_ref, out_ref, value):
    owners = out_ref.shape[0]
    coefs, leaves = sum_ref.shape
    whole = coefs // LANES * LANES

    @pl.when(pl.program_id(0) == 0)
    def _():
        mask = mask_ref[...]
        kind = lax.broadcasted_iota(jnp.int32, (8, leaves), 0)
        spot = lax.broadcasted_iota(jnp.int32, (8, leaves), 1)
        octant = jnp.where((spot & 7) == kind, mask, 0.0).astype(jnp.bfloat16)
        value[pl.ds(whole, LANES), :] = jnp.zeros((LANES, leaves), jnp.bfloat16)
        value[pl.ds(0, coefs), :] = (sum_ref[...] * mask).astype(jnp.bfloat16)
        value[pl.ds(whole + 32, 8), :] = octant

    row = lax.broadcasted_iota(jnp.int32, (owners * CAP, leaves), 0)
    at = row + pl.program_id(0) * (owners * CAP)
    pick = jnp.where(at == slot_ref[...], 1.0, 0.0).astype(jnp.bfloat16)
    main = lax.dot_general(
        pick, value[...], (((1,), (1,)), ((), ())), preferred_element_type=jnp.float32
    )
    for q in range(whole // LANES):
        block = main[:, q * LANES : (q + 1) * LANES].astype(jnp.bfloat16)
        out_ref[:, q * CAP : (q + 1) * CAP, :] = block.reshape(owners, CAP, LANES)
    rest = main[:, whole:].reshape(owners, CAP, LANES)
    moved = pltpu.roll(rest[:, 8:, :].reshape(owners * 8, LANES), 64, 1)
    rest = rest[:, :8, :] + moved.reshape(owners, 8, LANES) + parts_ref[...][None]
    out_ref[:, whole // LANES * CAP :, :] = rest.astype(jnp.bfloat16)


def send_call(slot, total, mask, parts, devices):
    coefs, leaves = total.shape
    owners = 32
    rows = coefs // LANES * CAP + 8
    whole = lambda x: pl.BlockSpec(x.shape, lambda s: (0, 0))
    return pl.pallas_call(
        send_kernel,
        out_shape=jax.ShapeDtypeStruct((devices, rows, LANES), jnp.bfloat16),
        grid=(devices // owners,),
        in_specs=[whole(x) for x in (slot, total, mask, parts)],
        out_specs=pl.BlockSpec((owners, rows, LANES), lambda s: (s, 0, 0)),
        scratch_shapes=[
            pltpu.VMEM((coefs // LANES * LANES + LANES, leaves), jnp.bfloat16),
        ],
        compiler_params=pltpu.CompilerParams(vmem_limit_bytes=60 * 2**20),
        cost_estimate=pl.CostEstimate(
            flops=2 * devices * CAP * 1024 * 768, bytes_accessed=8_000_000, transcendentals=0
        ),
        name="send",
    )(slot, total, mask, parts)


def split(x):
    high = x.astype(jnp.bfloat16)
    rest = x - high.astype(jnp.float32)
    middle = rest.astype(jnp.bfloat16)
    return high, middle, (rest - middle.astype(jnp.float32)).astype(jnp.bfloat16)


def advect_kernel(
    box_ref, values_ref, got_ref, parts_ref, first_ref, weights_ref, couple_ref, node_ref,
    down_ref, spread_ref, sum_ref, mask_ref, out_ref, vel_ref, table, far,
):
    nodes = out_ref.shape[1]
    owners = got_ref.shape[0]
    boxes = weights_ref.shape[0] // 6
    step = pl.program_id(0)

    @pl.when(step == 0)
    def _():
        sent = parts_ref[...].reshape(parts_ref.shape[0] * 8, LANES)
        mixed = jnp.dot(weights_ref[...], sent, preferred_element_type=jnp.float32)
        mixed = mixed.reshape(3, 2, boxes, LANES)
        mixed = mixed[0] + mixed[1] + mixed[2]
        mixed = jnp.concatenate([mixed[0], mixed[1]], axis=1)
        expansion = jnp.dot(
            mixed, couple_ref[...], precision=HIGH, preferred_element_type=jnp.float32
        )
        stacked = jnp.concatenate(
            [expansion[:, j * LANES : (j + 1) * LANES] for j in range(3)], axis=0
        )
        boxed = jnp.dot(
            stacked.astype(jnp.bfloat16), node_ref[...], preferred_element_type=jnp.float32
        ).astype(jnp.bfloat16)
        for j in range(3):
            for o in range(8):
                table[j, o * boxes : (o + 1) * boxes, :] = boxed[
                    j * boxes : (j + 1) * boxes, o * nodes : (o + 1) * nodes
                ]
        row = lax.broadcasted_iota(jnp.int32, (boxes, 3 * LANES), 0)
        mine = jnp.sum(jnp.where(row == box_ref[0], expansion, 0.0), axis=0, keepdims=True)
        own = jnp.concatenate(
            [jnp.broadcast_to(mine[:, j * LANES : (j + 1) * LANES], (8, LANES)) for j in range(3)]
            + [jnp.zeros((8, LANES), jnp.float32)],
            axis=0,
        )
        wide = jnp.dot(
            jnp.concatenate(split(own), axis=0), down_ref[...], preferred_element_type=jnp.float32
        )
        wide = wide[:32] + wide[32:64] + wide[64:]
        kind = lax.broadcasted_iota(jnp.int32, (8, 256), 0)
        for j in range(3):
            field = jnp.zeros((8, 256), jnp.float32)
            for o in range(8):
                part = wide[8 * j : 8 * (j + 1), o * 256 : (o + 1) * 256]
                field = field + jnp.where(kind == o, part, 0.0)
            far[j] = jnp.concatenate([field] * 16, axis=0).T

    width = vel_ref.shape[0] // 3
    for j in range(3):
        rows = pl.ds(j * width, width)
        shade = jnp.concatenate([far[j, pl.ds(0, width), :]] * (vel_ref.shape[1] // LANES), axis=1)
        vel_ref[rows, :] = ((sum_ref[rows, :] + shade) * mask_ref[...]).astype(jnp.bfloat16)

    tiles = [
        got_ref[:, q * CAP : (q + 1) * CAP, :].reshape(owners * CAP, LANES) for q in range(5)
    ]
    last = got_ref[:, 5 * CAP :, :].reshape(owners * 8, LANES)

    def times(left, start):
        right = first_ref[pl.ds(start, left.shape[1]), :]
        return jnp.dot(left, right, preferred_element_type=jnp.float32)

    def joined(halves):
        halves = [half.reshape(owners, 8, nodes) for half in halves]
        return jnp.concatenate(halves, axis=1).reshape(owners * CAP, nodes)

    octant = joined(
        [jnp.dot(last, spread_ref[b], preferred_element_type=jnp.float32) for b in range(2)]
    )
    lane = lax.broadcasted_iota(jnp.int32, octant.shape, 1) & (boxes - 1)
    place = lax.broadcasted_iota(jnp.int32, octant.shape, 0)
    place = lax.shift_right_logical(place, 6) + step * (owners // SPAN)
    choice = jnp.where(lane == place, octant, 0.0).astype(jnp.bfloat16)
    speeds = (
        times(jnp.concatenate(tiles[0:2], axis=1), 0),
        times(jnp.concatenate(tiles[1:4], axis=1), 256),
        times(jnp.concatenate(tiles[3:5], axis=1), 640)
        + joined([times(last, 896 + LANES * b) for b in range(2)]),
    )
    correction = None
    for j, speed in enumerate(speeds):
        speed = speed + jnp.dot(choice, table[j], preferred_element_type=jnp.float32)
        term = speed * values_ref[:, (j + 1) * nodes : (j + 2) * nodes].astype(jnp.float32)
        correction = term if correction is None else correction + term
    value = values_ref[:, :nodes].astype(jnp.float32)
    alive = jnp.max(octant, axis=1, keepdims=True)
    out_ref[...] = (alive * (value - TIME_STEP * correction)).astype(jnp.bfloat16)


def advect_call(box, values, got, first, weights, couple, node, down, spread, total, mask):
    slots = values.shape[0]
    nodes = values.shape[1] // 4
    coefs, leaves = total.shape
    rows = 512
    steps = slots // rows
    same = lambda x: pl.BlockSpec(x.shape, lambda s, b: (0,) * x.ndim)
    return pl.pallas_call(
        advect_kernel,
        out_shape=(
            jax.ShapeDtypeStruct((slots, nodes), jnp.bfloat16),
            jax.ShapeDtypeStruct((coefs, leaves), jnp.bfloat16),
        ),
        grid_spec=pltpu.PrefetchScalarGridSpec(
            num_scalar_prefetch=1,
            grid=(steps,),
            in_specs=[
                pl.BlockSpec((rows, values.shape[1]), lambda s, b: (s, 0)),
                pl.BlockSpec((rows // CAP,) + got.shape[1:], lambda s, b: (s, 0, 0)),
                pl.BlockSpec((got.shape[0], 8, LANES), lambda s, b: (0, 10, 0)),
            ]
            + [same(x) for x in (first, weights, couple, node, down, spread)]
            + [
                pl.BlockSpec((coefs, leaves // steps), lambda s, b: (0, s)),
                pl.BlockSpec((1, leaves // steps), lambda s, b: (0, s)),
            ],
            out_specs=(
                pl.BlockSpec((rows, nodes), lambda s, b: (s, 0)),
                pl.BlockSpec((coefs, leaves // steps), lambda s, b: (0, s)),
            ),
            scratch_shapes=[
                pltpu.VMEM((3, 256, nodes), jnp.bfloat16),
                pltpu.VMEM((3, 256, LANES), jnp.float32),
            ],
        ),
        compiler_params=pltpu.CompilerParams(vmem_limit_bytes=62 * 2**20),
        cost_estimate=pl.CostEstimate(
            flops=2 * slots * 256 * 2304, bytes_accessed=14_000_000, transcendentals=0
        ),
        name="advect",
    )(box, values, got, got, first, weights, couple, node, down, spread, total, mask)


def local(
    density,
    vel_mask,
    near_list,
    near_ops,
    upward_ops,
    coupling_operators,
    coarse_weights,
    downward_ops,
    conc_owner,
    concentration,
    departure,
    departure_class,
    shift_ops,
    eval_ops,
):
    leaves, width = density.shape
    positions = near_list.shape[1]
    devices = lax.axis_size("leaf")
    me = lax.axis_index("leaf")
    box = me // SPAN
    slots = concentration.shape[0]
    capacity = slots // devices
    nodes = eval_ops.shape[1] // 4
    forward = [(i, i + 1) for i in range(devices - 1)]
    backward = [(i + 1, i) for i in range(devices - 1)]

    alive = vel_mask.astype(jnp.float32)
    own = live_call(density.T, vel_mask[None, :])
    low = lax.ppermute(own, "leaf", forward)
    high = lax.ppermute(own, "leaf", backward)

    octant = (jnp.arange(leaves, dtype=jnp.int32)[:, None] % 8) == jnp.arange(8, dtype=jnp.int32)
    sums = jnp.dot(own.T, octant.astype(jnp.bfloat16), preferred_element_type=jnp.float32)[:width]
    part = jnp.einsum("po,opq->q", sums, upward_ops.astype(jnp.float32), precision=HIGH)

    owner = conc_owner[:, 0]
    named = (jnp.arange(devices, dtype=jnp.int32)[:, None] == owner[None, :]).astype(jnp.bfloat16)
    spot = jnp.arange(leaves, dtype=jnp.int32)
    before = (spot[:, None] < spot[None, :]).astype(jnp.bfloat16)
    count = jnp.dot(named, before, preferred_element_type=jnp.float32)
    rank = jnp.sum(count * named.astype(jnp.float32), axis=0).astype(jnp.int32)
    slot = (owner * capacity + rank)[None, :]
    high_part = lax.reduce_precision(part, 8, 7)
    middle_part = lax.reduce_precision(part - high_part, 8, 7)
    pieces = jnp.stack([high_part, middle_part, part - high_part - middle_part])
    none = lambda n: jnp.zeros((3, n), jnp.float32)
    even = jnp.concatenate([none(40), pieces[:, :24], none(40), pieces[:, 24:48]], axis=1)
    odd = jnp.concatenate([none(40), pieces[:, 48:], none(80)], axis=1)
    parts = jnp.pad(jnp.stack([even, odd], axis=1).reshape(6, LANES), ((0, 2), (0, 0)))

    rows = (near_list.T - me * leaves + leaves) * 2
    groups = (positions - 1) // NEAR_GROUP
    rows = jnp.concatenate([rows[:NEAR_GROUP], rows[NEAR_GROUP + 1 :]], axis=0)
    rows = rows.reshape(groups, NEAR_GROUP, leaves // NEAR_TILE, NEAR_TILE)
    rows = rows.transpose(2, 0, 1, 3).reshape(-1, NEAR_GROUP * NEAR_TILE)
    total = near_call(rows, low, own, high, near_ops.transpose(0, 2, 1))
    send = send_call(slot, total, alive[None, :], parts, devices)
    eval_ops, shift_ops, coarse_weights, coupling_operators, downward_ops, send = (
        lax.optimization_barrier(
            (eval_ops, shift_ops, coarse_weights, coupling_operators, downward_ops, send)
        )
    )
    got = lax.all_to_all(send, "leaf", split_axis=0, concat_axis=0, tiled=True)
    values = base_call(
        concentration.T,
        departure[None, :],
        departure_class[None, :],
        shift_ops.transpose(0, 2, 1),
        eval_ops,
    )

    one = eval_ops[:, :nodes]
    tail = 3 * width - 640
    starts = ((0, 0, width), (256 + width - 128, 0, width), (640 + 2 * width - 384, 0, width - tail))
    starts = starts + ((896, width - tail, tail), (896 + LANES + 64, width - tail, tail))
    target = jnp.arange(1152, dtype=jnp.int32)[:, None]
    source = jnp.arange(width, dtype=jnp.int32)[None, :]
    place = jnp.zeros((1152, width), bool)
    for at, origin, count in starts:
        inside = (target >= at) & (target < at + count)
        place = place | (inside & (target - at + origin == source))
    first = jnp.dot(place.astype(jnp.bfloat16), one, preferred_element_type=jnp.float32)
    first = first.astype(jnp.bfloat16)
    boxes = coarse_weights.shape[0]
    spot = jnp.arange(8 * devices, dtype=jnp.int32)
    wide = jnp.repeat(coarse_weights, 8 * SPAN, axis=1)
    wide_high = lax.reduce_precision(wide, 8, 7)
    wide_middle = lax.reduce_precision(wide - wide_high, 8, 7)
    wide = jnp.stack([wide_high, wide_middle, wide - wide_high - wide_middle])[:, None]
    parity = jnp.arange(2, dtype=jnp.int32)[None, :, None, None]
    used = (spot % 2 == parity) & (spot % 8 < 6)
    weights = jnp.where(used, wide, 0.0).reshape(6 * boxes, -1).astype(jnp.bfloat16)
    couple = jnp.pad(coupling_operators.reshape(-1, 3, 56), ((0, 0), (0, 0), (0, LANES - 56)))
    couple = couple.reshape(-1, 3 * LANES)
    blank = lambda n: jnp.zeros((n, 3 * LANES), jnp.float32)
    couple = jnp.concatenate(
        [blank(40), couple[:24], blank(40), couple[24:48], blank(40), couple[48:], blank(80)]
    )
    node = jnp.einsum(
        "oqp,pn->qon", downward_ops, one, preferred_element_type=jnp.float32
    ).reshape(56, 8 * nodes)
    node = jnp.pad(node, ((0, LANES - 56), (0, 0))).astype(jnp.bfloat16)
    down = jnp.pad(downward_ops.transpose(1, 0, 2), ((0, LANES - 56), (0, 0), (0, 256 - width)))
    down = down.reshape(LANES, 8 * 256)
    lane = jnp.arange(LANES, dtype=jnp.int32)[:, None]
    column = jnp.arange(8 * boxes, dtype=jnp.int32)[None, :] // boxes
    spread = jnp.stack([(lane == 32 + 64 * b + column) for b in range(2)]).astype(jnp.bfloat16)
    advected, velocity = advect_call(
        box[None].astype(jnp.int32), values, got, first, weights, couple, node, down, spread,
        total, alive[None, :],
    )
    return velocity.T, advected


def solution(mesh):
    placed = (
        P("leaf", None),
        P("leaf"),
        P("leaf", None),
        P(),
        P(),
        P(),
        P(),
        P(),
        P("leaf", None),
        P("leaf", None),
        P("leaf"),
        P("leaf"),
        P(),
        P(),
    )
    return jax.shard_map(
        local,
        mesh=mesh,
        in_specs=placed,
        out_specs=(P("leaf", None), P("leaf", None)),
        check_vma=False,
    )
```

```python
import jax
import jax.numpy as jnp
from jax import lax
from jax.experimental import pallas as pl
from jax.experimental.pallas import tpu as pltpu
from jax.sharding import PartitionSpec as P

SPAN = 4
TIME_STEP = 0.5
TILE = 256
LANES = 128
CAP = 16
NEAR_TILE = 512
NEAR_GROUP = 13
HIGH = lax.Precision.HIGHEST
VMEM = pl.BlockSpec(memory_space=pltpu.VMEM)


def live_kernel(density_ref, mask_ref, out_ref):
    width, leaves = density_ref.shape
    x = density_ref[...].astype(jnp.float32) * mask_ref[...].astype(jnp.float32)
    x = jnp.concatenate([x, jnp.zeros((256 - width, leaves), jnp.float32)], axis=0)
    out_ref[...] = x.T.astype(jnp.bfloat16)


def live_call(density, mask):
    return pl.pallas_call(
        live_kernel,
        out_shape=jax.ShapeDtypeStruct((density.shape[1], 256), jnp.bfloat16),
        grid=(density.shape[1] // TILE,),
        in_specs=[
            pl.BlockSpec((density.shape[0], TILE), lambda s: (0, s)),
            pl.BlockSpec((1, TILE), lambda s: (0, s)),
        ],
        out_specs=pl.BlockSpec((TILE, 256), lambda s: (s, 0)),
        compiler_params=pltpu.CompilerParams(vmem_limit_bytes=62 * 2**20),
        name="live",
    )(density, mask)


def near_kernel(
    idx_hbm, low_hbm, own_hbm, high_hbm, ops_hbm, out_hbm,
    table, picked, parts, ops, sums, idx_a, idx_b, idx_sem, part_sem, ops_sem, out_sem,
):
    positions, _, width = ops.shape
    leaves = parts.shape[1]
    group = picked.shape[0]
    groups = (positions - 1) // group
    center = group
    steps = leaves // NEAR_TILE * groups
    half = idx_a.shape[0] // NEAR_TILE

    def fetch_a(k):
        return pltpu.make_async_copy(
            idx_hbm.at[k, pl.ds(0, half * NEAR_TILE)], idx_a, idx_sem.at[0]
        )

    def fetch_b(k):
        return pltpu.make_async_copy(
            idx_hbm.at[k, pl.ds(half * NEAR_TILE, (group - half) * NEAR_TILE)],
            idx_b,
            idx_sem.at[1],
        )

    def fetch_ops(k):
        rows = pl.ds(k * (group + 1), group)
        return pltpu.make_async_copy(ops_hbm.at[rows], ops.at[rows], ops_sem.at[k])

    middle = pltpu.make_async_copy(ops_hbm.at[center], ops.at[center], ops_sem.at[groups])

    def contract_rows(position, rows):
        return lax.dot_general(
            ops[position], rows, (((1,), (1,)), ((), ())), preferred_element_type=jnp.float32
        )

    order = ((1, own_hbm), (0, low_hbm), (2, high_hbm))
    copies = [pltpu.make_async_copy(ref, parts.at[p], part_sem.at[p]) for p, ref in order]
    copies[0].start()
    middle.start()
    fetch_a(0).start()
    fetch_b(0).start()
    for copy in copies[1:]:
        copy.start()
    for k in range(groups):
        fetch_ops(k).start()
    picked[group - 1] = jnp.zeros((2 * NEAR_TILE, LANES), jnp.float32)
    for (part, _), copy in zip(order, copies):
        copy.wait()

        def fill(s, c, part=part):
            x = parts[part, pl.ds(pl.multiple_of(s * TILE, TILE), TILE), :].astype(jnp.float32)
            start = part * 2 * leaves + s * 2 * TILE
            table[pl.ds(start, TILE, stride=2), :] = x[:, :LANES]
            table[pl.ds(start + 1, TILE, stride=2), :] = x[:, LANES:]
            return c

        lax.fori_loop(0, leaves // TILE, fill, 0)
        if part == 1:
            middle.wait()
            for tile in range(leaves // NEAR_TILE):
                rows = parts[1, pl.ds(tile * NEAR_TILE, NEAR_TILE), :][:, :width]
                sums[tile] = contract_rows(center, rows)

    def product(t, position):
        first = picked[t, pl.ds(0, NEAR_TILE, stride=2), :].astype(jnp.bfloat16)
        second = picked[t, pl.ds(1, NEAR_TILE, stride=2), :].astype(jnp.bfloat16)
        return contract_rows(position, jnp.concatenate([first, second], axis=1)[:, :width])

    def store(tile):
        cols = pl.ds(pl.multiple_of(tile * NEAR_TILE, NEAR_TILE), NEAR_TILE)
        return pltpu.make_async_copy(sums.at[tile], out_hbm.at[:, cols], out_sem.at[tile])

    def step(s, c):
        tile = lax.div(s, groups)
        g = s - tile * groups
        last = lax.max(s - 1, 0)
        last_tile = lax.div(last, groups)
        last_position = (last - last_tile * groups) * (group + 1) + group - 1
        later = lax.min(s + 1, steps - 1)

        @pl.when(s < groups)
        def _():
            fetch_ops(s).wait()

        @pl.when((g == 1) & (tile > 0))
        def _():
            store(tile - 1).start()

        fetch_a(0).wait()
        total = None
        for t in range(group):
            if t == half:
                fetch_a(later).start()
                fetch_b(0).wait()
            for i in range(NEAR_TILE):
                at = t * NEAR_TILE + i
                row = idx_a[at] if t < half else idx_b[at - half * NEAR_TILE]
                picked[t, pl.ds(2 * i, 2), :] = table[pl.ds(pl.multiple_of(row, 2), 2), :]
            if t == 0:
                sums[last_tile] += product(group - 1, last_position)
            else:
                term = product(t - 1, g * (group + 1) + t - 1)
                total = term if total is None else total + term
        fetch_b(later).start()
        sums[tile] += total
        return c

    tiles = leaves // NEAR_TILE
    lax.fori_loop(0, steps, step, 0)
    sums[tiles - 1] += product(group - 1, positions - 1)
    store(tiles - 1).start()
    for tile in range(tiles):
        store(tile).wait()
    fetch_a(0).wait()
    fetch_b(0).wait()


def near_call(idx, low, own, high, ops):
    positions, coefs, width = ops.shape
    leaves = own.shape[0]
    half = (NEAR_GROUP + 1) // 2
    anywhere = pl.BlockSpec(memory_space=pl.ANY)
    return pl.pallas_call(
        near_kernel,
        out_shape=jax.ShapeDtypeStruct((coefs, leaves), jnp.float32),
        in_specs=[anywhere] * 5,
        out_specs=anywhere,
        scratch_shapes=[
            pltpu.VMEM((6 * leaves, LANES), jnp.float32),
            pltpu.VMEM((NEAR_GROUP, 2 * NEAR_TILE, LANES), jnp.float32),
            pltpu.VMEM((3,) + own.shape, jnp.bfloat16),
            pltpu.VMEM(ops.shape, jnp.bfloat16),
            pltpu.VMEM((leaves // NEAR_TILE, coefs, NEAR_TILE), jnp.float32),
            pltpu.SMEM((half * NEAR_TILE,), jnp.int32),
            pltpu.SMEM(((NEAR_GROUP - half) * NEAR_TILE,), jnp.int32),
            pltpu.SemaphoreType.DMA((2,)),
            pltpu.SemaphoreType.DMA((3,)),
            pltpu.SemaphoreType.DMA(((positions - 1) // NEAR_GROUP + 1,)),
            pltpu.SemaphoreType.DMA((leaves // NEAR_TILE,)),
        ],
        compiler_params=pltpu.CompilerParams(
            vmem_limit_bytes=60 * 2**20,
        ),
        cost_estimate=pl.CostEstimate(
            flops=2 * positions * leaves * 256 * 1024, bytes_accessed=20_000_000, transcendentals=0
        ),
        name="near",
    )(idx, low, own, high, ops)


def base_kernel(conc_ref, dep_ref, cls_ref, shift_ref, eval_ref, out_ref):
    slots = conc_ref.shape[1]
    rows = lax.broadcasted_iota(jnp.int32, (slots, TILE), 0)
    pick = jnp.where(rows == dep_ref[...], 1.0, 0.0).astype(jnp.bfloat16)
    got = jnp.dot(conc_ref[...], pick, preferred_element_type=jnp.float32)
    kind = cls_ref[...]
    total = None
    for c in range(shift_ref.shape[0]):
        part = jnp.where(kind == c, got, 0.0).astype(jnp.bfloat16)
        term = jnp.dot(shift_ref[c], part, preferred_element_type=jnp.float32)
        total = term if total is None else total + term
    base = total.astype(jnp.bfloat16)
    out_ref[...] = lax.dot_general(
        base, eval_ref[...], (((0,), (0,)), ((), ())), preferred_element_type=jnp.float32
    ).astype(jnp.bfloat16)


def base_call(conc, dep, cls, shift, evals):
    width, slots = conc.shape
    return pl.pallas_call(
        base_kernel,
        out_shape=jax.ShapeDtypeStruct((slots, evals.shape[1]), jnp.bfloat16),
        grid=(slots // TILE,),
        in_specs=[
            pl.BlockSpec(conc.shape, lambda s: (0, 0)),
            pl.BlockSpec((1, TILE), lambda s: (0, s)),
            pl.BlockSpec((1, TILE), lambda s: (0, s)),
            pl.BlockSpec(shift.shape, lambda s: (0, 0, 0)),
            pl.BlockSpec(evals.shape, lambda s: (0, 0)),
        ],
        out_specs=pl.BlockSpec((TILE, evals.shape[1]), lambda s: (s, 0)),
        compiler_params=pltpu.CompilerParams(vmem_limit_bytes=62 * 2**20),
        cost_estimate=pl.CostEstimate(
            flops=2 * slots * 256 * 4096, bytes_accessed=3_000_000, transcendentals=0
        ),
        name="base",
    )(conc, dep, cls, shift, evals)


def send_kernel(slot_ref, sum_ref, mask_ref, parts_ref, out_ref, value):
    owners = out_ref.shape[0]
    coefs, leaves = sum_ref.shape
    whole = coefs // LANES * LANES

    @pl.when(pl.program_id(0) == 0)
    def _():
        mask = mask_ref[...]
        kind = lax.broadcasted_iota(jnp.int32, (8, leaves), 0)
        spot = lax.broadcasted_iota(jnp.int32, (8, leaves), 1)
        octant = jnp.where((spot & 7) == kind, mask, 0.0).astype(jnp.bfloat16)
        value[pl.ds(whole, LANES), :] = jnp.zeros((LANES, leaves), jnp.bfloat16)
        value[pl.ds(0, coefs), :] = (sum_ref[...] * mask).astype(jnp.bfloat16)
        value[pl.ds(whole + 32, 8), :] = octant

    row = lax.broadcasted_iota(jnp.int32, (owners * CAP, leaves), 0)
    at = row + pl.program_id(0) * (owners * CAP)
    pick = jnp.where(at == slot_ref[...], 1.0, 0.0).astype(jnp.bfloat16)
    main = lax.dot_general(
        pick, value[...], (((1,), (1,)), ((), ())), preferred_element_type=jnp.float32
    )
    for q in range(whole // LANES):
        block = main[:, q * LANES : (q + 1) * LANES].astype(jnp.bfloat16)
        out_ref[:, q * CAP : (q + 1) * CAP, :] = block.reshape(owners, CAP, LANES)
    rest = main[:, whole:].reshape(owners, CAP, LANES)
    moved = pltpu.roll(rest[:, 8:, :].reshape(owners * 8, LANES), 64, 1)
    rest = rest[:, :8, :] + moved.reshape(owners, 8, LANES) + parts_ref[...][None]
    out_ref[:, whole // LANES * CAP :, :] = rest.astype(jnp.bfloat16)


def send_call(slot, total, mask, parts, devices):
    coefs, leaves = total.shape
    owners = 32
    rows = coefs // LANES * CAP + 8
    whole = lambda x: pl.BlockSpec(x.shape, lambda s: (0, 0))
    return pl.pallas_call(
        send_kernel,
        out_shape=jax.ShapeDtypeStruct((devices, rows, LANES), jnp.bfloat16),
        grid=(devices // owners,),
        in_specs=[whole(x) for x in (slot, total, mask, parts)],
        out_specs=pl.BlockSpec((owners, rows, LANES), lambda s: (s, 0, 0)),
        scratch_shapes=[
            pltpu.VMEM((coefs // LANES * LANES + LANES, leaves), jnp.bfloat16),
        ],
        compiler_params=pltpu.CompilerParams(vmem_limit_bytes=60 * 2**20),
        cost_estimate=pl.CostEstimate(
            flops=2 * devices * CAP * 1024 * 768, bytes_accessed=8_000_000, transcendentals=0
        ),
        name="send",
    )(slot, total, mask, parts)


def split(x):
    high = x.astype(jnp.bfloat16)
    rest = x - high.astype(jnp.float32)
    middle = rest.astype(jnp.bfloat16)
    return high, middle, (rest - middle.astype(jnp.float32)).astype(jnp.bfloat16)


def advect_kernel(
    box_ref, values_ref, got_ref, parts_ref, first_ref, weights_ref, couple_ref, node_ref,
    down_ref, spread_ref, sum_ref, mask_ref, out_ref, vel_ref, table, far,
):
    nodes = out_ref.shape[1]
    owners = got_ref.shape[0]
    boxes = weights_ref.shape[0] // 6
    step = pl.program_id(0)

    @pl.when(step == 0)
    def _():
        sent = parts_ref[...].reshape(parts_ref.shape[0] * 8, LANES)
        mixed = jnp.dot(weights_ref[...], sent, preferred_element_type=jnp.float32)
        mixed = mixed.reshape(3, 2, boxes, LANES)
        mixed = mixed[0] + mixed[1] + mixed[2]
        mixed = jnp.concatenate([mixed[0], mixed[1]], axis=1)
        expansion = jnp.dot(
            mixed, couple_ref[...], precision=HIGH, preferred_element_type=jnp.float32
        )
        stacked = jnp.concatenate(
            [expansion[:, j * LANES : (j + 1) * LANES] for j in range(3)], axis=0
        )
        boxed = jnp.dot(
            stacked.astype(jnp.bfloat16), node_ref[...], preferred_element_type=jnp.float32
        ).astype(jnp.bfloat16)
        for j in range(3):
            for o in range(8):
                table[j, o * boxes : (o + 1) * boxes, :] = boxed[
                    j * boxes : (j + 1) * boxes, o * nodes : (o + 1) * nodes
                ]
        row = lax.broadcasted_iota(jnp.int32, (boxes, 3 * LANES), 0)
        mine = jnp.sum(jnp.where(row == box_ref[0], expansion, 0.0), axis=0, keepdims=True)
        own = jnp.concatenate(
            [jnp.broadcast_to(mine[:, j * LANES : (j + 1) * LANES], (8, LANES)) for j in range(3)]
            + [jnp.zeros((8, LANES), jnp.float32)],
            axis=0,
        )
        wide = jnp.dot(
            jnp.concatenate(split(own), axis=0), down_ref[...], preferred_element_type=jnp.float32
        )
        wide = wide[:32] + wide[32:64] + wide[64:]
        kind = lax.broadcasted_iota(jnp.int32, (8, 256), 0)
        for j in range(3):
            field = jnp.zeros((8, 256), jnp.float32)
            for o in range(8):
                part = wide[8 * j : 8 * (j + 1), o * 256 : (o + 1) * 256]
                field = field + jnp.where(kind == o, part, 0.0)
            far[j] = jnp.concatenate([field] * 16, axis=0).T

    width = vel_ref.shape[0] // 3
    for j in range(3):
        rows = pl.ds(j * width, width)
        shade = jnp.concatenate([far[j, pl.ds(0, width), :]] * (vel_ref.shape[1] // LANES), axis=1)
        vel_ref[rows, :] = ((sum_ref[rows, :] + shade) * mask_ref[...]).astype(jnp.bfloat16)

    tiles = [
        got_ref[:, q * CAP : (q + 1) * CAP, :].reshape(owners * CAP, LANES) for q in range(5)
    ]
    last = got_ref[:, 5 * CAP :, :].reshape(owners * 8, LANES)

    def times(left, start):
        right = first_ref[pl.ds(start, left.shape[1]), :]
        return jnp.dot(left, right, preferred_element_type=jnp.float32)

    def joined(halves):
        halves = [half.reshape(owners, 8, nodes) for half in halves]
        return jnp.concatenate(halves, axis=1).reshape(owners * CAP, nodes)

    octant = joined(
        [jnp.dot(last, spread_ref[b], preferred_element_type=jnp.float32) for b in range(2)]
    )
    lane = lax.broadcasted_iota(jnp.int32, octant.shape, 1) & (boxes - 1)
    place = lax.broadcasted_iota(jnp.int32, octant.shape, 0)
    place = lax.shift_right_logical(place, 6) + step * (owners // SPAN)
    choice = jnp.where(lane == place, octant, 0.0).astype(jnp.bfloat16)
    speeds = (
        times(jnp.concatenate(tiles[0:2], axis=1), 0),
        times(jnp.concatenate(tiles[1:4], axis=1), 256),
        times(jnp.concatenate(tiles[3:5], axis=1), 640)
        + joined([times(last, 896 + LANES * b) for b in range(2)]),
    )
    correction = None
    for j, speed in enumerate(speeds):
        speed = speed + jnp.dot(choice, table[j], preferred_element_type=jnp.float32)
        term = speed * values_ref[:, (j + 1) * nodes : (j + 2) * nodes].astype(jnp.float32)
        correction = term if correction is None else correction + term
    value = values_ref[:, :nodes].astype(jnp.float32)
    alive = jnp.max(octant, axis=1, keepdims=True)
    out_ref[...] = (alive * (value - TIME_STEP * correction)).astype(jnp.bfloat16)


def advect_call(box, values, got, first, weights, couple, node, down, spread, total, mask):
    slots = values.shape[0]
    nodes = values.shape[1] // 4
    coefs, leaves = total.shape
    rows = 512
    steps = slots // rows
    same = lambda x: pl.BlockSpec(x.shape, lambda s, b: (0,) * x.ndim)
    return pl.pallas_call(
        advect_kernel,
        out_shape=(
            jax.ShapeDtypeStruct((slots, nodes), jnp.bfloat16),
            jax.ShapeDtypeStruct((coefs, leaves), jnp.bfloat16),
        ),
        grid_spec=pltpu.PrefetchScalarGridSpec(
            num_scalar_prefetch=1,
            grid=(steps,),
            in_specs=[
                pl.BlockSpec((rows, values.shape[1]), lambda s, b: (s, 0)),
                pl.BlockSpec((rows // CAP,) + got.shape[1:], lambda s, b: (s, 0, 0)),
                pl.BlockSpec((got.shape[0], 8, LANES), lambda s, b: (0, 10, 0)),
            ]
            + [same(x) for x in (first, weights, couple, node, down, spread)]
            + [
                pl.BlockSpec((coefs, leaves // steps), lambda s, b: (0, s)),
                pl.BlockSpec((1, leaves // steps), lambda s, b: (0, s)),
            ],
            out_specs=(
                pl.BlockSpec((rows, nodes), lambda s, b: (s, 0)),
                pl.BlockSpec((coefs, leaves // steps), lambda s, b: (0, s)),
            ),
            scratch_shapes=[
                pltpu.VMEM((3, 256, nodes), jnp.bfloat16),
                pltpu.VMEM((3, 256, LANES), jnp.float32),
            ],
        ),
        compiler_params=pltpu.CompilerParams(vmem_limit_bytes=62 * 2**20),
        cost_estimate=pl.CostEstimate(
            flops=2 * slots * 256 * 2304, bytes_accessed=14_000_000, transcendentals=0
        ),
        name="advect",
    )(box, values, got, got, first, weights, couple, node, down, spread, total, mask)


def local(
    density,
    vel_mask,
    near_list,
    near_ops,
    upward_ops,
    coupling_operators,
    coarse_weights,
    downward_ops,
    conc_owner,
    concentration,
    departure,
    departure_class,
    shift_ops,
    eval_ops,
):
    leaves, width = density.shape
    positions = near_list.shape[1]
    devices = lax.axis_size("leaf")
    me = lax.axis_index("leaf")
    box = me // SPAN
    slots = concentration.shape[0]
    capacity = slots // devices
    nodes = eval_ops.shape[1] // 4
    forward = [(i, i + 1) for i in range(devices - 1)]
    backward = [(i + 1, i) for i in range(devices - 1)]

    alive = vel_mask.astype(jnp.float32)
    own = live_call(density.T, vel_mask[None, :])
    low = lax.ppermute(own, "leaf", forward)
    high = lax.ppermute(own, "leaf", backward)

    octant = (jnp.arange(leaves, dtype=jnp.int32)[:, None] % 8) == jnp.arange(8, dtype=jnp.int32)
    sums = jnp.dot(own.T, octant.astype(jnp.bfloat16), preferred_element_type=jnp.float32)[:width]
    part = jnp.einsum("po,opq->q", sums, upward_ops.astype(jnp.float32), precision=HIGH)

    owner = conc_owner[:, 0]
    named = (jnp.arange(devices, dtype=jnp.int32)[:, None] == owner[None, :]).astype(jnp.bfloat16)
    spot = jnp.arange(leaves, dtype=jnp.int32)
    before = (spot[:, None] < spot[None, :]).astype(jnp.bfloat16)
    count = jnp.dot(named, before, preferred_element_type=jnp.float32)
    rank = jnp.sum(count * named.astype(jnp.float32), axis=0).astype(jnp.int32)
    slot = (owner * capacity + rank)[None, :]
    high_part = lax.reduce_precision(part, 8, 7)
    middle_part = lax.reduce_precision(part - high_part, 8, 7)
    pieces = jnp.stack([high_part, middle_part, part - high_part - middle_part])
    none = lambda n: jnp.zeros((3, n), jnp.float32)
    even = jnp.concatenate([none(40), pieces[:, :24], none(40), pieces[:, 24:48]], axis=1)
    odd = jnp.concatenate([none(40), pieces[:, 48:], none(80)], axis=1)
    parts = jnp.pad(jnp.stack([even, odd], axis=1).reshape(6, LANES), ((0, 2), (0, 0)))

    rows = (near_list.T - me * leaves + leaves) * 2
    groups = (positions - 1) // NEAR_GROUP
    rows = jnp.concatenate([rows[:NEAR_GROUP], rows[NEAR_GROUP + 1 :]], axis=0)
    rows = rows.reshape(groups, NEAR_GROUP, leaves // NEAR_TILE, NEAR_TILE)
    rows = rows.transpose(2, 0, 1, 3).reshape(-1, NEAR_GROUP * NEAR_TILE)
    total = near_call(rows, low, own, high, near_ops.transpose(0, 2, 1))
    send = send_call(slot, total, alive[None, :], parts, devices)
    eval_ops, shift_ops, coarse_weights, coupling_operators, downward_ops, send = (
        lax.optimization_barrier(
            (eval_ops, shift_ops, coarse_weights, coupling_operators, downward_ops, send)
        )
    )
    got = lax.all_to_all(send, "leaf", split_axis=0, concat_axis=0, tiled=True)
    values = base_call(
        concentration.T,
        departure[None, :],
        departure_class[None, :],
        shift_ops.transpose(0, 2, 1),
        eval_ops,
    )

    one = eval_ops[:, :nodes]
    tail = 3 * width - 640
    starts = ((0, 0, width), (256 + width - 128, 0, width), (640 + 2 * width - 384, 0, width - tail))
    starts = starts + ((896, width - tail, tail), (896 + LANES + 64, width - tail, tail))
    target = jnp.arange(1152, dtype=jnp.int32)[:, None]
    source = jnp.arange(width, dtype=jnp.int32)[None, :]
    place = jnp.zeros((1152, width), bool)
    for at, origin, count in starts:
        inside = (target >= at) & (target < at + count)
        place = place | (inside & (target - at + origin == source))
    first = jnp.dot(place.astype(jnp.bfloat16), one, preferred_element_type=jnp.float32)
    first = first.astype(jnp.bfloat16)
    boxes = coarse_weights.shape[0]
    spot = jnp.arange(8 * devices, dtype=jnp.int32)
    wide = jnp.repeat(coarse_weights, 8 * SPAN, axis=1)
    wide_high = lax.reduce_precision(wide, 8, 7)
    wide_middle = lax.reduce_precision(wide - wide_high, 8, 7)
    wide = jnp.stack([wide_high, wide_middle, wide - wide_high - wide_middle])[:, None]
    parity = jnp.arange(2, dtype=jnp.int32)[None, :, None, None]
    used = (spot % 2 == parity) & (spot % 8 < 6)
    weights = jnp.where(used, wide, 0.0).reshape(6 * boxes, -1).astype(jnp.bfloat16)
    couple = jnp.pad(coupling_operators.reshape(-1, 3, 56), ((0, 0), (0, 0), (0, LANES - 56)))
    couple = couple.reshape(-1, 3 * LANES)
    blank = lambda n: jnp.zeros((n, 3 * LANES), jnp.float32)
    couple = jnp.concatenate(
        [blank(40), couple[:24], blank(40), couple[24:48], blank(40), couple[48:], blank(80)]
    )
    node = jnp.einsum(
        "oqp,pn->qon", downward_ops, one, preferred_element_type=jnp.float32
    ).reshape(56, 8 * nodes)
    node = jnp.pad(node, ((0, LANES - 56), (0, 0))).astype(jnp.bfloat16)
    down = jnp.pad(downward_ops.transpose(1, 0, 2), ((0, LANES - 56), (0, 0), (0, 256 - width)))
    down = down.reshape(LANES, 8 * 256)
    lane = jnp.arange(LANES, dtype=jnp.int32)[:, None]
    column = jnp.arange(8 * boxes, dtype=jnp.int32)[None, :] // boxes
    spread = jnp.stack([(lane == 32 + 64 * b + column) for b in range(2)]).astype(jnp.bfloat16)
    advected, velocity = advect_call(
        box[None].astype(jnp.int32), values, got, first, weights, couple, node, down, spread,
        total, alive[None, :],
    )
    return velocity.T, advected


def solution(mesh):
    placed = (
        P("leaf", None),
        P("leaf"),
        P("leaf", None),
        P(),
        P(),
        P(),
        P(),
        P(),
        P("leaf", None),
        P("leaf", None),
        P("leaf"),
        P("leaf"),
        P(),
        P(),
    )
    return jax.shard_map(
        local,
        mesh=mesh,
        in_specs=placed,
        out_specs=(P("leaf", None), P("leaf", None)),
        check_vma=False,
    )
```
